512 devices in a mesh: lat: 16 (over y, core), lon: 32 (over x, z).
Axes of the slice: x: 4, y: 8, z: 8, core: 2. Of those that a mesh axis runs over, the one named last changes fastest.
Arguments:
- latent: bfloat16 [32, 384, 640], P('lat', 'lon'), may hold values from -6 to 6
- lon_filter: bfloat16 [9, 384], replicated, may hold values from -0.3125 to 0.3125
- mix_weight: bfloat16 [9, 640, 20], P(None, 'lon'), may hold values from -1.25 to 1.25
- band_weight: bfloat16 [9, 32, 3], P(None, 'lat'), may hold values from -1.25 to 1.25
- offsets: int32 [32], P('lat'), may hold values from -2 to 31, as said below
- w_up: bfloat16 [640, 1280], replicated, may hold values from -0.25 to 0.25
- w_down: bfloat16 [1280, 640], replicated, may hold values from -0.15625 to 0.15625
Outputs:
- result: bfloat16 [32, 384, 640], P('lat', 'lon')
The draws below stay inside these ranges and needn't reach their ends.
Inputs may be any that keep to these rules, and one draw needn't show every extreme that they name: offsets[i] - i lies between -2 and 0, so a band's rows lie within 2 rows of its output row; in every aligned block of 2 rows the first row's band starts 2 rows below it and the last row's band ends 2 rows above it.
All inputs are finite; a program needn't handle non-finite values.
Results may differ from the reference program's by a relative error of at most 0.0095.
Values may be sent and summed in bfloat16 or wider, within the bound.
A program may use at most 128 MiB of HBM per device.

```python
import jax
import jax.numpy as jnp
from jax import lax

C = 640
HID = 1280
GROUP = 20
NB = 9
BW = 3
REACH = 2
LAT_DEV = 2
LAT = 32
LON = 384


def draw_offsets(key, part):
    top_shift = 2 * REACH - BW + 1
    shifts = jax.random.randint(jax.random.fold_in(key, 17), (LAT,), 0, top_shift + 1).astype(jnp.int32)
    places = jnp.arange(LAT, dtype=jnp.int32)
    within = places % LAT_DEV
    shifts = jnp.where(within == 0, 0, shifts)
    shifts = jnp.where(within == LAT_DEV - 1, top_shift, shifts)
    return (places - REACH + shifts).astype(jnp.int32)


def steps_of(key, shape, split, smallest, top_value):
    def one(position, parts):
        steps = jax.random.uniform(jax.random.fold_in(jax.random.fold_in(key, 6), position), (parts,), jnp.float32, smallest / len(split), top_value / len(split))
        return jnp.repeat(jnp.exp(steps), shape[position] // parts).reshape((-1,) + (1,) * (len(shape) - position - 1))

    level = one(*split[0])
    for cut in split[1:]:
        level = level * one(*cut)
    return level


def scatter_about(own_key, dims, scale, most, cuts=(), kind=jnp.bfloat16):
    drawn = jax.random.normal(own_key, dims, jnp.float32) * scale
    if len(cuts) > 0:
        drawn = steps_of(own_key, dims, cuts, -0.22, 0.18) * drawn
    return jnp.clip(drawn, min=-most, max=most).astype(kind)


def setup_inputs(seed: int = 0) -> dict:
    key_of = jax.random.split(jax.random.key(seed), 8)
    return {
        "latent": scatter_about(key_of[0], (LAT, LON, C), 1.0, 6.0, ((0, 16), (1, 32))),
        "lon_filter": scatter_about(key_of[1], (NB, LON), LON ** -0.5, 0.3125),
        "mix_weight": scatter_about(key_of[2], (NB, C, GROUP), GROUP ** -0.5, 1.25, ((1, 32),)),
        "band_weight": scatter_about(key_of[3], (NB, LAT, BW), (NB * BW) ** -0.5, 1.25, ((1, 16),)),
        "offsets": draw_offsets(jax.random.fold_in(key_of[7], 71), 0),
        "w_up": scatter_about(key_of[5], (C, HID), C ** -0.5, 0.25),
        "w_down": scatter_about(key_of[6], (HID, C), HID ** -0.5, 0.15625),
    }


def circulant(lon_filter):
    length = lon_filter.shape[1]
    places = jnp.arange(length, dtype=jnp.int32)
    index_table = (places[:, None] - places[None, :]) % length
    return lon_filter[:, index_table]

def block_mix(mix_weight):
    chan_width = mix_weight.shape[1]
    group_size = mix_weight.shape[2]
    repeated = jnp.tile(mix_weight.astype(jnp.float32), (1, 1, chan_width // group_size))
    member = jnp.arange(chan_width, dtype=jnp.int32) // group_size
    same_group = (member[:, None] == member[None, :]).astype(jnp.float32)
    return repeated * same_group[None]

def feed_forward(summed, w_up, w_down):
    flat_rows = summed.reshape(-1, summed.shape[-1]).astype(jnp.float32)
    row_mean = lax.optimization_barrier(jnp.mean(flat_rows, axis=1, keepdims=True))
    centred = flat_rows - row_mean
    row_var = lax.optimization_barrier(jnp.mean(centred * centred, axis=1, keepdims=True))
    normed = (centred * lax.rsqrt(row_var + 1e-05)).astype(jnp.bfloat16)
    hidden = jax.nn.gelu(jnp.dot(normed, w_up, preferred_element_type=jnp.float32), approximate=False).astype(jnp.bfloat16)
    output = flat_rows + jnp.dot(hidden, w_down, preferred_element_type=jnp.float32)
    return output.astype(jnp.bfloat16).reshape(summed.shape)

def reference(latent, lon_filter, mix_weight, band_weight, offsets, w_up, w_down):
    latent_f = latent.astype(jnp.float32)
    lon_table = circulant(lon_filter).astype(jnp.float32)
    mix_blocks = block_mix(mix_weight)
    band_f = band_weight.astype(jnp.float32)

    def one_basis(running, inputs):
        table_k, block_k, band_k = inputs
        spread = jnp.einsum('ijc,xj->icx', latent_f, table_k, precision=lax.Precision.HIGHEST)
        mixed_rows = jnp.einsum('icx,dc->idx', spread, block_k, precision=lax.Precision.HIGHEST).astype(jnp.bfloat16)
        padded = jnp.pad(mixed_rows, ((REACH, REACH), (0, 0), (0, 0)))
        for band_tap in range(BW):
            picked = (offsets + band_tap + REACH).astype(jnp.int32)
            running = running + band_k[:, band_tap][:, None, None] * padded[picked].astype(jnp.float32)
        return (running, None)
    convolved, unused = lax.scan(one_basis, jnp.zeros((LAT, C, LON), jnp.float32), (lon_table, mix_blocks, band_f))
    convolved = convolved.astype(jnp.bfloat16)
    turned = jnp.transpose(convolved, (0, 2, 1)).astype(jnp.float32)
    summed = (latent_f + turned).astype(jnp.bfloat16)
    return feed_forward(summed, w_up, w_down)
```

```python
import jax
import jax.numpy as jnp
from jax import lax
from jax.experimental import pallas as pl
from jax.experimental.pallas import tpu as pltpu
from jax.sharding import PartitionSpec as P

BW = 3
REACH = 2


def extended(block, sides, width):
    for axis, dim in sides:
        count = lax.axis_size(axis)
        forward = [(i, i + 1) for i in range(count - 1)]
        backward = [(target, source) for source, target in forward]
        low = lax.ppermute(
            lax.slice_in_dim(block, block.shape[dim] - width, None, axis=dim), axis, forward
        )
        high = lax.ppermute(lax.slice_in_dim(block, 0, width, axis=dim), axis, backward)
        block = jnp.concatenate([low, block, high], axis=dim)
    return block


def circulant_kernel(filter_ref, table_ref):
    length = filter_ref.shape[1]
    for k in range(filter_ref.shape[0]):
        row = filter_ref[k : k + 1, :].astype(jnp.float32)
        spread_row = jnp.broadcast_to(row, (length, length))
        turned = pltpu.roll(spread_row, 0, 1, stride=1, stride_axis=0)
        table_ref[k] = turned.astype(jnp.bfloat16)


def circulant(lon_filter):
    count, length = lon_filter.shape
    return pl.pallas_call(
        circulant_kernel,
        out_shape=jax.ShapeDtypeStruct((count, length, length), jnp.bfloat16),
    )(lon_filter)


def block_mix(mix_weight):
    chan_width = mix_weight.shape[1]
    group_size = mix_weight.shape[2]
    repeated = jnp.tile(mix_weight.astype(jnp.float32), (1, 1, chan_width // group_size))
    member = jnp.arange(chan_width, dtype=jnp.int32) // group_size
    same_group = (member[:, None] == member[None, :]).astype(jnp.float32)
    return repeated * same_group[None]


def feed_forward(summed, w_up, w_down):
    flat_rows = summed.reshape(-1, summed.shape[-1]).astype(jnp.float32)
    row_mean = jnp.mean(flat_rows, axis=1, keepdims=True)
    centred = flat_rows - row_mean
    row_var = jnp.mean(centred * centred, axis=1, keepdims=True)
    normed = (centred * lax.rsqrt(row_var + 1e-05)).astype(jnp.bfloat16)
    hidden = jax.nn.gelu(
        jnp.dot(normed, w_up, preferred_element_type=jnp.float32), approximate=False
    ).astype(jnp.bfloat16)
    output = flat_rows + jnp.dot(hidden, w_down, preferred_element_type=jnp.float32)
    return output.astype(jnp.bfloat16).reshape(summed.shape)


def local(latent, lon_filter, mix_weight, band_weight, offsets, w_up, w_down):
    lat_dev = latent.shape[0]
    grouped = lax.all_to_all(latent, "lon", split_axis=2, concat_axis=1, tiled=True)
    lon_table = circulant(lon_filter)
    mix_blocks = block_mix(mix_weight)
    spread = lax.dot_general(
        grouped, lon_table, (((1,), (1,)), ((), ())), preferred_element_type=jnp.float32
    )
    mixed_rows = extended(
        jnp.einsum("rckx,kdc->rkdx", spread, mix_blocks, precision=lax.Precision.HIGHEST).astype(
            jnp.bfloat16
        ),
        (("lat", 0),),
        REACH,
    )
    first_row = lax.axis_index("lat") * lat_dev
    rim_span = lat_dev + 2 * REACH
    positions = offsets[:, None] + jnp.arange(BW, dtype=jnp.int32)[None, :] - first_row + REACH
    onehot = (positions[:, :, None] == jnp.arange(rim_span, dtype=jnp.int32)[None, None, :]).astype(
        jnp.float32
    )
    band_dense = jnp.einsum(
        "kit,itr->kir", band_weight.astype(jnp.float32), onehot, precision=lax.Precision.HIGHEST
    ).astype(jnp.bfloat16)
    convolved = jnp.einsum(
        "kir,rkdx->idx", band_dense, mixed_rows, preferred_element_type=jnp.float32
    ).astype(jnp.bfloat16)
    returned = lax.all_to_all(convolved, "lon", split_axis=2, concat_axis=1, tiled=True)
    turned = jnp.transpose(returned, (0, 2, 1)).astype(jnp.float32)
    summed = (latent.astype(jnp.float32) + turned).astype(jnp.bfloat16)
    return feed_forward(summed, w_up, w_down)


def solution(mesh):
    return jax.shard_map(
        local,
        mesh=mesh,
        in_specs=(
            P("lat", "lon", None),
            P(),
            P(None, "lon", None),
            P(None, "lat", None),
            P("lat"),
            P(),
            P(),
        ),
        out_specs=P("lat", "lon", None),
        check_vma=False,
    )
```

```python
import jax
import jax.numpy as jnp
from jax import lax
from jax.experimental import pallas as pl
from jax.experimental.pallas import tpu as pltpu
from jax.sharding import PartitionSpec as P

MESH = pl.DeviceIdType.MESH
F32 = jnp.float32
BF16 = jnp.bfloat16
X_CHIPS, Z_CHIPS = 4, 8
LANES = 128
SLOT = 32
AHEAD = 8


def peers():
    steps = [(dx, dz) for dx in range(X_CHIPS) for dz in range(Z_CHIPS) if dx or dz]
    return sorted(steps, key=lambda s: -(min(s[0], X_CHIPS - s[0]) + min(s[1], Z_CHIPS - s[1])))


def lane_index(rows=8):
    return lax.broadcasted_iota(jnp.int32, (rows, LANES), 1)


def erf_gelu(value):
    return 0.5 * value * (1.0 + lax.erf(value * 0.7071067811865476))


def kernel(
    latent_hbm, filter_hbm, mix_hbm, band_hbm, up_hbm, down_hbm, out_ref,
    latent_in, filter_in, mix_in, band_in, up_in, down_in,
    rows, parts_out, parts_own, parts_low, parts_high, back_out, back_in,
    gathered, stack, table, mix_wide, mixer, turned,
    load_sem, out_sem, own_sem, low_sem, high_sem, halo_sem, back_send_sem, back_sem,
):
    lat, lon = lax.axis_index("lat"), lax.axis_index("lon")
    lats, lons = lax.axis_size("lat"), lax.axis_size("lon")
    width = latent_in.shape[1]
    channels = latent_in.shape[2]
    group = mix_in.shape[2]
    count, length = filter_in.shape
    my_x, my_z = lon // Z_CHIPS, lon % Z_CHIPS
    others = [
        lax.rem(my_x + dx, X_CHIPS) * Z_CHIPS + lax.rem(my_z + dz, Z_CHIPS) for dx, dz in peers()
    ]
    has_low, has_high = lat > 0, lat < lats - 1

    barrier = pltpu.get_barrier_semaphore()
    for other in others:
        pl.semaphore_signal(barrier, inc=1, device_id=(lat, other), device_id_type=MESH)

    @pl.when(has_low)
    def _():
        pl.semaphore_signal(barrier, inc=1, device_id=(lat - 1, lon), device_id_type=MESH)

    @pl.when(has_high)
    def _():
        pl.semaphore_signal(barrier, inc=1, device_id=(lat + 1, lon), device_id_type=MESH)

    loads = [
        pltpu.make_async_copy(source, target, load_sem.at[n])
        for n, (source, target) in enumerate(
            (
                (latent_hbm, latent_in),
                (filter_hbm, filter_in),
                (mix_hbm, mix_in),
                (band_hbm, band_in),
                (up_hbm, up_in),
                (down_hbm, down_in),
            )
        )
    ]
    for load in loads:
        load.start()

    rows[...] = jnp.zeros(rows.shape, F32)
    loads[0].wait()
    for i in range(2):
        values = latent_in[i].astype(F32)
        rows[8 * i : 8 * i + 8, :] = values[0:AHEAD]
        rows[16 + 8 * i : 16 + 8 * i + width - AHEAD, :] = values[AHEAD:width]

    lane = lane_index()
    odd = lax.rem(lon, 2) == 1
    tiles = [rows[8 * q : 8 * q + 8, :] for q in range(4)]
    for q in (2, 3):
        tiles[q] = jnp.where(odd, pltpu.roll(tiles[q], 4, 0), tiles[q])
    for g in range(channels // group):
        tile, place = divmod(g * group, LANES)
        message = jnp.zeros((8, LANES), F32)
        for q in range(4):
            piece = tiles[q][:, tile * LANES : (tile + 1) * LANES]
            if place + group > LANES:
                after = tiles[q][:, (tile + 1) * LANES : (tile + 2) * LANES]
                piece = jnp.where(lane >= place, piece, after)
            shift = (SLOT * q - place) % LANES
            if shift:
                piece = pltpu.roll(piece, shift, 1)
            inside = (lane >= SLOT * q) & (lane < SLOT * q + group)
            message = jnp.where(inside, piece, message)
        parts_out[g] = message.astype(BF16)
    parts_own[lon] = parts_out[lon]

    pl.semaphore_wait(
        barrier, lons - 1 + has_low.astype(jnp.int32) + has_high.astype(jnp.int32)
    )

    def send(source, target, send_sem, recv_sem, device):
        return pltpu.make_async_remote_copy(
            src_ref=source,
            dst_ref=target,
            send_sem=send_sem,
            recv_sem=recv_sem,
            device_id=device,
            device_id_type=MESH,
        )

    for other in others:
        send(parts_out.at[other], parts_own.at[lon], out_sem, own_sem, (lat, other)).start()

    loads[1].wait()
    row16 = lax.broadcasted_iota(jnp.int32, (8, length), 0)
    filters = filter_in[...].astype(F32)
    for k in range(count):
        first = jnp.broadcast_to(filters[k : k + 1, :], (8, length))
        first = pltpu.roll(first, 0, 1, stride=1, stride_axis=0)
        last = jnp.where(row16 < 4, pltpu.roll(first, AHEAD, 1), pltpu.roll(first, 2 * AHEAD, 1))
        first = jnp.concatenate([first, pltpu.roll(first, width, 1)], axis=0)
        last = jnp.concatenate([last, pltpu.roll(last, 2 * width, 1)], axis=0)
        base = k * length
        for p in range(lons // 2):
            turn = pltpu.roll(first, 2 * width * p, 1) if p else first
            table[base + 16 * p : base + 16 * p + 16, :] = turn.astype(BF16)
        base += 8 * lons
        for p in range(lons // 4):
            turn = pltpu.roll(last, 4 * width * p, 1) if p else last
            table[base + 16 * p : base + 16 * p + 16, :] = turn.astype(BF16)

    loads[2].wait()
    loads[3].wait()
    mix_wide[...] = jnp.zeros(mix_wide.shape, F32)
    slot = lax.broadcasted_iota(jnp.int32, (1, LANES), 1) // SLOT
    for k in range(count):
        mix_wide[k, 0:group, 0:group] = mix_in[k].astype(F32)
        once = mix_wide[k]
        all_slots = once
        for q in range(1, 4):
            all_slots = all_slots + pltpu.roll(once, SLOT * q, 1)
        bands = band_in[k].astype(F32)
        band = [[bands[i : i + 1, t : t + 1] for t in range(3)] for i in range(2)]

        def lanes_of(values):
            scale = jnp.zeros((1, LANES), F32)
            for q, value in values:
                scale = jnp.where(slot == q, value, scale)
            return (all_slots * scale).astype(BF16)

        top, end = 2 * SLOT * k, 2 * SLOT * k + SLOT
        mixer[top : top + SLOT, 0:LANES] = lanes_of([(0, band[0][0]), (1, band[0][1]), (2, band[0][2])])
        mixer[top : top + SLOT, LANES:] = jnp.zeros((SLOT, LANES), BF16)
        mixer[end : end + SLOT, 0:LANES] = lanes_of([(3, band[1][0])])
        mixer[end : end + SLOT, LANES:] = lanes_of([(0, band[1][1]), (1, band[1][2])])

    turned[length:, :] = jnp.zeros((turned.shape[0] - length, LANES), F32)
    stack[6 * SLOT :, :] = jnp.zeros((2 * SLOT, length), BF16)

    others_count = lons - 1
    some = send(
        parts_out.at[pl.ds(0, others_count)], parts_own.at[pl.ds(0, others_count)], out_sem, own_sem, (lat, others[0])
    )
    some.wait_recv()
    to_low = send(parts_own, parts_high, halo_sem.at[0], high_sem, (lat - 1, lon))
    to_high = send(parts_own, parts_low, halo_sem.at[1], low_sem, (lat + 1, lon))

    @pl.when(has_low)
    def _():
        to_low.start()

    @pl.when(has_high)
    def _():
        to_high.start()

    def unfold(parts, row):
        for b in range(lons):
            gathered[8 * b : 8 * b + 8, :] = parts[b].astype(F32)
        half = gathered[...]
        first = half.T[0 : 2 * SLOT, :]
        pairs = half.reshape(lons // 2, 2, 8, LANES)
        last = (pairs[:, 0] + pairs[:, 1]).reshape(4 * lons, LANES).T[2 * SLOT : 4 * SLOT, :]
        stack[row : row + 2 * SLOT, 0 : 8 * lons] = first.astype(BF16)
        stack[row : row + 2 * SLOT, 8 * lons :] = last.astype(BF16)

    unfold(parts_own, 2 * SLOT)

    @pl.when(has_low)
    def _():
        to_high.wait_recv()
        unfold(parts_low, 0)

    @pl.when(jnp.logical_not(has_low))
    def _():
        stack[0 : 2 * SLOT, :] = jnp.zeros((2 * SLOT, length), BF16)

    @pl.when(has_high)
    def _():
        to_low.wait_recv()
        unfold(parts_high, 4 * SLOT)

    @pl.when(jnp.logical_not(has_high))
    def _():
        stack[4 * SLOT : 6 * SLOT, :] = jnp.zeros((2 * SLOT, length), BF16)

    mixed = jnp.dot(mixer[...], stack[...], preferred_element_type=F32).astype(BF16)
    side = jnp.concatenate([mixed[2 * SLOT * k : 2 * SLOT * (k + 1), :] for k in range(count)], axis=1)
    convolved = jnp.dot(side, table[...], preferred_element_type=F32)
    turned[0:length, :] = jnp.concatenate([convolved, convolved], axis=0).T

    for b in range(lons):
        start = turned[width * b : width * b + 8, :]
        rest = turned[width * b + AHEAD : width * b + AHEAD + 8, :]
        back_out[b] = jnp.where(lane < 2 * SLOT, start, rest).astype(BF16)
    back_in[lon] = back_out[lon]
    for other in others:
        send(back_out.at[other], back_in.at[lon], back_send_sem, back_sem, (lat, other)).start()

    loads[4].wait()
    loads[5].wait()
    last = send(
        back_out.at[pl.ds(0, others_count)], back_in.at[pl.ds(0, others_count)], back_send_sem, back_sem, (lat, others[0])
    )
    last.wait_recv()

    blocks = channels // LANES
    sums = [[jnp.zeros((8, LANES), F32) for _ in range(blocks)] for _ in range(4)]
    for g in range(channels // group):
        tile, place = divmod(g * group, LANES)
        message = back_in[g].astype(F32)
        for q in range(4):
            shift = (place - SLOT * q) % LANES
            piece = pltpu.roll(message, shift, 1) if shift else message
            inside = (lane >= place) & (lane < place + group)
            sums[q][tile] = jnp.where(inside, piece, sums[q][tile])
            if place + group > LANES:
                sums[q][tile + 1] = jnp.where(lane < place + group - LANES, piece, sums[q][tile + 1])
    turned_back = jnp.concatenate([jnp.concatenate(one, axis=1) for one in sums], axis=0)

    summed = (rows[...] + turned_back).astype(BF16).astype(F32)
    mean = jnp.mean(summed, axis=1, keepdims=True)
    centred = summed - mean
    var = jnp.mean(centred * centred, axis=1, keepdims=True)
    normed = (centred * lax.rsqrt(var + 1e-05)).astype(BF16)
    hidden = erf_gelu(jnp.dot(normed, up_in[...], preferred_element_type=F32)).astype(BF16)
    result = summed + jnp.dot(hidden, down_in[...], preferred_element_type=F32)
    result = result.astype(BF16)
    for i in range(2):
        out_ref[i, 0:AHEAD, :] = result[8 * i : 8 * i + 8]
        out_ref[i, AHEAD:width, :] = result[16 + 8 * i : 16 + 8 * i + width - AHEAD]

    some.wait_send()
    last.wait_send()

    @pl.when(has_low)
    def _():
        to_low.wait_send()

    @pl.when(has_high)
    def _():
        to_high.wait_send()


def local(latent, lon_filter, mix_weight, band_weight, offsets, w_up, w_down):
    del offsets
    count, length = lon_filter.shape
    lons = lax.axis_size("lon")
    channels, hidden = w_up.shape
    parts = pltpu.VMEM((lons, 8, LANES), BF16)
    whole = pl.BlockSpec(memory_space=pl.ANY)
    return pl.pallas_call(
        kernel,
        out_shape=jax.ShapeDtypeStruct(latent.shape, latent.dtype),
        in_specs=[whole] * 6,
        out_specs=pl.BlockSpec(memory_space=pltpu.VMEM),
        scratch_shapes=[
            pltpu.VMEM(latent.shape, BF16),
            pltpu.VMEM(lon_filter.shape, BF16),
            pltpu.VMEM(mix_weight.shape, BF16),
            pltpu.VMEM(band_weight.shape, BF16),
            pltpu.VMEM(w_up.shape, BF16),
            pltpu.VMEM(w_down.shape, BF16),
            pltpu.VMEM((4 * 8, channels), F32),
            parts,
            parts,
            parts,
            parts,
            parts,
            parts,
            pltpu.VMEM((8 * lons, LANES), F32),
            pltpu.VMEM((8 * SLOT, length), BF16),
            pltpu.VMEM((count * length, length), BF16),
            pltpu.VMEM((count, SLOT, LANES), F32),
            pltpu.VMEM((count * 2 * SLOT, 8 * SLOT), BF16),
            pltpu.VMEM((length + 8, LANES), F32),
            pltpu.SemaphoreType.DMA((6,)),
            pltpu.SemaphoreType.DMA,
            pltpu.SemaphoreType.DMA,
            pltpu.SemaphoreType.DMA,
            pltpu.SemaphoreType.DMA,
            pltpu.SemaphoreType.DMA((2,)),
            pltpu.SemaphoreType.DMA,
            pltpu.SemaphoreType.DMA,
        ],
        compiler_params=pltpu.CompilerParams(collective_id=0, has_side_effects=True),
    )(latent, lon_filter, mix_weight, band_weight, w_up, w_down)


def solution(mesh):
    return jax.shard_map(
        local,
        mesh=mesh,
        in_specs=(
            P("lat", "lon", None),
            P(),
            P(None, "lon", None),
            P(None, "lat", None),
            P("lat"),
            P(),
            P(),
        ),
        out_specs=P("lat", "lon", None),
        check_vma=False,
    )
```

```python
import jax
import jax.numpy as jnp
from jax import lax
from jax.experimental import pallas as pl
from jax.experimental.pallas import tpu as pltpu
from jax.sharding import PartitionSpec as P

MESH = pl.DeviceIdType.MESH
F32 = jnp.float32
BF16 = jnp.bfloat16
X_CHIPS, Z_CHIPS = 4, 8
WORK_Z = (6, 7, 0, 1)
WORKERS = X_CHIPS * len(WORK_Z)
WORK_LON = [x * Z_CHIPS + z for x in range(X_CHIPS) for z in WORK_Z]
LANES = 128
AHEAD = 8


def erf_gelu(value):
    return 0.5 * value * (1.0 + lax.erf(value * 0.7071067811865476))


def kernel(
    latent_hbm, filter_hbm, mix_hbm, band_hbm, up_hbm, down_hbm, out_ref,
    latent_in, filter_in, mix_in, band_in, up_in, down_in,
    points, rows, parts_out, parts_in, back_out, back_in,
    gathered, ends, stack, table, mix_wide, mixer, turned, turned_last,
    load_sem, small_send_sem, mix_sem, band_sem, out_sem, side_sem, in_sem, back_send_sem, back_sem,
):
    lat, lon = lax.axis_index("lat"), lax.axis_index("lon")
    lats, lons = lax.axis_size("lat"), lax.axis_size("lon")
    width, _, channels = latent_in.shape
    count, length = filter_in.shape
    group = mix_in.shape[3]
    share = channels // WORKERS
    core = lax.rem(lat, 2)
    base = lat - core
    my_x, my_z = lon // Z_CHIPS, lax.rem(lon, Z_CHIPS)
    my_turn = lax.rem(my_z + Z_CHIPS - WORK_Z[0], Z_CHIPS)
    my_work = my_x * len(WORK_Z) + my_turn
    work_chip = my_turn < len(WORK_Z)
    works = work_chip & (core == 1)
    idle = jnp.logical_not(works)
    has_low, has_high = base > 0, base + 2 < lats
    aside = base + jnp.where(core == 0, -1, 3)
    has_side = jnp.where(core == 0, base > 0, base + 2 < lats)

    def load(source, target, n):
        return pltpu.make_async_copy(source, target, load_sem.at[n])

    latent_load = load(latent_hbm, latent_in, 0)
    filter_load = load(filter_hbm, filter_in, 1)
    band_load = load(band_hbm, band_in.at[1], 2)
    up_load = load(up_hbm, up_in, 3)
    down_load = load(down_hbm, down_in, 4)
    latent_load.start()

    def send(source, target, send_sem, recv_sem, device):
        return pltpu.make_async_remote_copy(
            src_ref=source,
            dst_ref=target,
            send_sem=send_sem,
            recv_sem=recv_sem,
            device_id=device,
            device_id_type=MESH,
        )

    barrier = pltpu.get_barrier_semaphore()

    def signal(to_lat, to_lon):
        pl.semaphore_signal(barrier, inc=1, device_id=(to_lat, to_lon), device_id_type=MESH)

    @pl.when(works)
    def _():
        for z in reversed(range(Z_CHIPS)):
            for x in range(X_CHIPS):
                signal(base, x * Z_CHIPS + z)

        @pl.when(has_high)
        def _():
            for z in reversed(range(Z_CHIPS)):
                for x in range(X_CHIPS):
                    signal(base + 2, x * Z_CHIPS + z)

        for n in range(1, lons):
            signal(base + 1, lax.rem(lon + n, lons))

        @pl.when(has_low)
        def _():
            for z in reversed(range(Z_CHIPS)):
                for x in range(X_CHIPS):
                    signal(base - 1, x * Z_CHIPS + z)

    filter_load.start()
    band_load.start()

    blocks = channels // LANES
    columns = [slice(LANES * t, LANES * (t + 1)) for t in range(blocks)]
    rest = width - AHEAD
    places = [
        (slice(0, AHEAD), pl.ds(0, AHEAD, stride=2)),
        (slice(AHEAD, 2 * AHEAD), pl.ds(1, AHEAD, stride=2)),
        (slice(2 * AHEAD, 2 * AHEAD + rest), pl.ds(2 * AHEAD, rest, stride=2)),
        (slice(2 * AHEAD + rest, 2 * width), pl.ds(2 * AHEAD + 1, rest, stride=2)),
    ]
    latent_load.wait()
    for t, column in enumerate(columns):
        for n in range(width):
            points[t, 2 * n : 2 * n + 2, :] = latent_in[n, :, column].astype(F32)
        for place, point in places:
            rows[place, column] = points[t, point, :]

    lane = lax.broadcasted_iota(jnp.int32, (8, LANES), 1)
    upper = lax.broadcasted_iota(jnp.int32, (8, LANES), 0) < rest
    tiles = [rows[8 * q : 8 * q + 8, :] for q in range(3)]
    tiles[2] = jnp.where(lax.rem(lon, 2) == 1, pltpu.roll(tiles[2], rest, 0), tiles[2])
    for w in range(WORKERS):
        tile, place = divmod(w * share, LANES)
        message = jnp.zeros((8, LANES), F32)
        for q in range(3):
            piece = tiles[q][:, columns[tile]]
            if place + share > LANES:
                piece = jnp.where(lane >= place, piece, tiles[q][:, columns[tile + 1]])
            shift = (share * q - place) % LANES
            if shift:
                piece = pltpu.roll(piece, shift, 1)
            inside = (lane >= share * q) & (lane < share * (q + 1))
            message = jnp.where(inside, piece, message)
        parts_out[w] = message.astype(BF16)

    @pl.when(works)
    def _():
        parts_in[2, lon] = parts_out[my_work]

    pl.semaphore_wait(
        barrier,
        WORKERS - works.astype(jnp.int32) + jnp.where(has_side, WORKERS, 0),
    )

    mix_work = lon // 2
    mix_lon = (mix_work // len(WORK_Z)) * Z_CHIPS + lax.rem(lax.rem(mix_work, len(WORK_Z)) + WORK_Z[0], Z_CHIPS)
    half = lax.rem(lon, 2)
    mix_send = send(mix_hbm, mix_in.at[half], small_send_sem, mix_sem.at[half], (lat, mix_lon))
    mix_copy = pltpu.make_async_copy(mix_hbm, mix_in.at[half], mix_sem.at[half])
    band_send = send(band_hbm, band_in.at[0], small_send_sem, band_sem, (base + 1, lon))
    mix_away = (core == 1) & (mix_lon != lon)
    band_away = (core == 0) & work_chip

    @pl.when(band_away)
    def _():
        band_send.start()

    @pl.when(mix_away)
    def _():
        mix_send.start()

    @pl.when((core == 1) & (mix_lon == lon))
    def _():
        mix_copy.start()

    @pl.when(has_side)
    def _():
        slot = jnp.where(core == 0, 3, 0)
        for w, to_lon in enumerate(WORK_LON):
            send(parts_out.at[w], parts_in.at[slot, lon], side_sem, in_sem.at[slot], (aside, to_lon)).start()

    for w, to_lon in enumerate(WORK_LON):

        @pl.when(jnp.logical_not(works & (my_work == w)))
        def _(w=w, to_lon=to_lon):
            send(parts_out.at[w], parts_in.at[core + 1, lon], out_sem, in_sem.at[core + 1], (base + 1, to_lon)).start()

    up_load.start()
    down_load.start()
    filter_load.wait()
    band_load.wait()

    @pl.when(works)
    def _():
        row8 = lax.broadcasted_iota(jnp.int32, (8, length), 0)
        filters = filter_in[...].astype(F32)
        for k in range(count):
            first = jnp.broadcast_to(filters[k : k + 1, :], (8, length))
            first = pltpu.roll(first, 0, 1, stride=1, stride_axis=0)
            last = jnp.where(row8 < rest, pltpu.roll(first, AHEAD, 1), pltpu.roll(first, 2 * AHEAD, 1))
            first = jnp.concatenate([first, pltpu.roll(first, width, 1)], axis=0)
            last = jnp.concatenate([last, pltpu.roll(last, 2 * width, 1)], axis=0)
            top = k * length
            for p in range(lons // 2):
                turn = pltpu.roll(first, 2 * width * p, 1) if p else first
                table[top + 16 * p : top + 16 * p + 16, :] = turn.astype(BF16)
            top += 8 * lons
            for p in range(lons // 4):
                turn = pltpu.roll(last, 4 * width * p, 1) if p else last
                table[top + 16 * p : top + 16 * p + 16, :] = turn.astype(BF16)

        mix_wide[...] = jnp.zeros(mix_wide.shape, F32)
        for h in range(2):
            send(mix_hbm, mix_in.at[h], small_send_sem, mix_sem.at[h], (lat, 0)).wait_recv()
        send(band_hbm, band_in.at[0], small_send_sem, band_sem, (base, lon)).wait_recv()
        third = lax.broadcasted_iota(jnp.int32, (1, LANES), 1) // share
        lower = lax.broadcasted_iota(jnp.int32, (share, LANES), 0) >= group
        bands = [band_in[o].astype(F32) for o in range(2)]
        empty = jnp.zeros((share, LANES), F32)
        for k in range(count):
            for h in range(2):
                mix_wide[group * h : group * (h + 1), 0:group] = mix_in[h, k].astype(F32)
            once = mix_wide[...]
            once = jnp.where(lower, pltpu.roll(once, group, 1), once)
            every = once + pltpu.roll(once, share, 1) + pltpu.roll(once, 2 * share, 1)
            for o in range(2):
                scaled = []
                for i in range(2):
                    scale = jnp.zeros((1, LANES), F32)
                    for t in range(3):
                        scale = jnp.where(third == t, bands[o][t, i : i + 1, k : k + 1], scale)
                    scaled.append(every * scale)
                whole = jnp.concatenate(
                    [
                        jnp.concatenate([scaled[0], empty], axis=1),
                        jnp.concatenate([empty, scaled[1]], axis=1),
                    ],
                    axis=0,
                )
                mixer[o, 2 * share * k : 2 * share * (k + 1), :] = whole.astype(BF16)

        turned[:, length:, :] = jnp.zeros((2, turned.shape[1] - length, LANES), F32)

        def unfold(n):
            for b in range(lons):
                gathered[8 * b : 8 * b + 8, :] = parts_in[n, b].astype(F32)
            for p in range(lons // 2):
                even, odd = gathered[16 * p : 16 * p + 8, :], gathered[16 * p + 8 : 16 * p + 16, :]
                one = pltpu.roll(jnp.where(upper, odd, even), rest, 0)
                one = pltpu.roll(one, LANES - 2 * share, 1)
                ends[8 * p : 8 * p + 8, :] = jnp.where(lane >= 2 * share, jnp.where(upper, even, odd), one)
            first, last = gathered[...].T, ends[...].T
            top = 2 * share * n
            stack[top : top + 2 * share, 0 : 8 * lons] = first[0 : 2 * share]
            stack[top : top + share, 8 * lons :] = last[2 * share : 3 * share]
            stack[top + share : top + 2 * share, 8 * lons :] = last[0:share]

        def arrive(n, members):
            taken = parts_in.at[n, pl.ds(0, members)]
            send(taken, taken, out_sem, in_sem.at[n], (lat, 0)).wait_recv()

        for n, there in ((0, has_low), (3, has_high)):

            @pl.when(there)
            def _(n=n):
                arrive(n, lons)
                unfold(n)

            @pl.when(jnp.logical_not(there))
            def _(n=n):
                stack[2 * share * n : 2 * share * (n + 1), :] = jnp.zeros((2 * share, length), F32)

        arrive(2, lons - 1)
        unfold(2)
        arrive(1, lons)
        unfold(1)

        pad = jnp.zeros((LANES - 3 * share, length), F32)
        sides = []
        for o in range(2):
            top = 2 * share * o
            wide = jnp.concatenate(
                [stack[top : top + 3 * share, :], pad, stack[top + 3 * share : top + 6 * share, :], pad], axis=0
            ).astype(BF16)
            mixed = jnp.dot(mixer[o], wide, preferred_element_type=F32).astype(BF16)
            sides.append(
                jnp.concatenate([mixed[2 * share * k : 2 * share * (k + 1), :] for k in range(count)], axis=1)
            )
        convolved = jnp.dot(jnp.concatenate(sides, axis=0), table[...], preferred_element_type=F32)

        for o in range(2):
            one = convolved[2 * share * o : 2 * share * (o + 1), :]
            one = jnp.concatenate([one, one[0:share], pad], axis=0).T
            turned[o, 0:length, :] = one
            turned_last[o] = pltpu.roll(one, share, 1)
        order = sorted(range(lons), key=lambda b: b % Z_CHIPS)
        for b in order:
            for o in (1, 0):
                start = turned[o, width * b : width * b + 8, :]
                end0 = turned[o, width * b + AHEAD : width * b + AHEAD + 8, :]
                end1 = turned_last[o, width * b + rest : width * b + rest + 8, :]
                message = jnp.where(lane < 2 * share, start, jnp.where(upper, end0, end1))
                back_out[o, b] = message.astype(BF16)
        back_in[my_work] = back_out[1, lon]
        for b in order:

            @pl.when(lon != b)
            def _(b=b):
                send(back_out.at[1, b], back_in.at[my_work], back_send_sem.at[1], back_sem, (base + 1, b)).start()

            send(back_out.at[0, b], back_in.at[my_work], back_send_sem.at[0], back_sem, (base, b)).start()

    def sent(buffer, members, sem):
        taken = buffer.at[pl.ds(0, members)]
        send(taken, taken, sem, back_sem, (lat, 0)).wait_send()

    def returned(members):
        taken = back_in.at[pl.ds(0, members)]
        send(taken, taken, out_sem, back_sem, (lat, 0)).wait_recv()

    up_load.wait()
    down_load.wait()

    @pl.when(works)
    def _():
        returned(WORKERS - 1)

    @pl.when(idle)
    def _():
        returned(WORKERS)

    sums = [[jnp.zeros((8, LANES), F32) for _ in range(blocks)] for _ in range(3)]
    for w in range(WORKERS):
        tile, place = divmod(w * share, LANES)
        message = back_in[w].astype(F32)
        for q in range(3):
            shift = (place - share * q) % LANES
            piece = pltpu.roll(message, shift, 1) if shift else message
            inside = (lane >= place) & (lane < place + share)
            sums[q][tile] = jnp.where(inside, piece, sums[q][tile])
            if place + share > LANES:
                sums[q][tile + 1] = jnp.where(lane < place + share - LANES, piece, sums[q][tile + 1])
    returned_rows = jnp.concatenate([jnp.concatenate(one, axis=1) for one in sums], axis=0)

    summed = (rows[...] + returned_rows).astype(BF16).astype(F32)
    mean = jnp.mean(summed, axis=1, keepdims=True)
    centred = summed - mean
    var = jnp.mean(centred * centred, axis=1, keepdims=True)
    normed = (centred * lax.rsqrt(var + 1e-05)).astype(BF16)
    hidden = erf_gelu(jnp.dot(normed, up_in[...], preferred_element_type=F32)).astype(BF16)
    result = summed + jnp.dot(hidden, down_in[...], preferred_element_type=F32)
    for t, column in enumerate(columns):
        for place, point in places:
            points[t, point, :] = result[place, column]
        for n in range(width):
            out_ref[n, :, column] = points[t, 2 * n : 2 * n + 2, :].astype(BF16)

    @pl.when(works)
    def _():
        sent(parts_out, WORKERS - 1, out_sem)
        sent(back_out.at[1], lons - 1, back_send_sem.at[1])
        sent(back_out.at[0], lons, back_send_sem.at[0])

    @pl.when(idle)
    def _():
        sent(parts_out, WORKERS, out_sem)

    @pl.when(has_side)
    def _():
        sent(parts_out, WORKERS, side_sem)

    @pl.when(mix_away)
    def _():
        mix_send.wait_send()

    @pl.when(band_away)
    def _():
        band_send.wait_send()


def local(latent, lon_filter, mix_weight, band_weight, offsets, w_up, w_down):
    del offsets
    latent, band_weight = jnp.transpose(latent, (1, 0, 2)), jnp.transpose(band_weight, (2, 1, 0))
    count, length = lon_filter.shape
    lons = lax.axis_size("lon")
    channels = w_up.shape[0]
    share = channels // WORKERS
    whole = pl.BlockSpec(memory_space=pl.ANY)
    result = pl.pallas_call(
        kernel,
        out_shape=jax.ShapeDtypeStruct(latent.shape, latent.dtype),
        in_specs=[whole] * 6,
        out_specs=pl.BlockSpec(memory_space=pltpu.VMEM),
        scratch_shapes=[
            pltpu.VMEM(latent.shape, BF16),
            pltpu.VMEM(lon_filter.shape, BF16),
            pltpu.VMEM((2, *mix_weight.shape), BF16),
            pltpu.VMEM((2, *band_weight.shape), BF16),
            pltpu.VMEM(w_up.shape, BF16),
            pltpu.VMEM(w_down.shape, BF16),
            pltpu.VMEM((channels // LANES, 2 * latent.shape[0], LANES), F32),
            pltpu.VMEM((2 * latent.shape[0], channels), F32),
            pltpu.VMEM((WORKERS, 8, LANES), BF16),
            pltpu.VMEM((4, lons, 8, LANES), BF16),
            pltpu.VMEM((2, lons, 8, LANES), BF16),
            pltpu.VMEM((WORKERS, 8, LANES), BF16),
            pltpu.VMEM((8 * lons, LANES), F32),
            pltpu.VMEM((4 * lons, LANES), F32),
            pltpu.VMEM((8 * share, length), F32),
            pltpu.VMEM((count * length, length), BF16),
            pltpu.VMEM((share, LANES), F32),
            pltpu.VMEM((2, count * 2 * share, 2 * LANES), BF16),
            pltpu.VMEM((2, length + 8, LANES), F32),
            pltpu.VMEM((2, length, LANES), F32),
            pltpu.SemaphoreType.DMA((5,)),
            pltpu.SemaphoreType.DMA,
            pltpu.SemaphoreType.DMA((2,)),
            pltpu.SemaphoreType.DMA,
            pltpu.SemaphoreType.DMA,
            pltpu.SemaphoreType.DMA,
            pltpu.SemaphoreType.DMA((4,)),
            pltpu.SemaphoreType.DMA((2,)),
            pltpu.SemaphoreType.DMA,
        ],
        compiler_params=pltpu.CompilerParams(collective_id=0, has_side_effects=True),
    )(latent, lon_filter, mix_weight, band_weight, w_up, w_down)
    return jnp.transpose(result, (1, 0, 2))


def solution(mesh):
    return jax.shard_map(
        local,
        mesh=mesh,
        in_specs=(
            P("lat", "lon", None),
            P(),
            P(None, "lon", None),
            P(None, "lat", None),
            P("lat"),
            P(),
            P(),
        ),
        out_specs=P("lat", "lon", None),
        check_vma=False,
    )
```

```python
import jax
import jax.numpy as jnp
from jax import lax
from jax.experimental import pallas as pl
from jax.experimental.pallas import tpu as pltpu
from jax.sharding import PartitionSpec as P

MESH = pl.DeviceIdType.MESH
F32 = jnp.float32
BF16 = jnp.bfloat16
X_CHIPS, Z_CHIPS = 4, 8
WORK_Z = 2
WORKERS = X_CHIPS * WORK_Z * 2
WORK_AT = [(core, x * Z_CHIPS + z) for x in range(X_CHIPS) for z in range(WORK_Z) for core in range(2)]
LANES = 128
AHEAD = 8


def erf_gelu(value):
    return 0.5 * value * (1.0 + lax.erf(value * 0.7071067811865476))


def kernel(
    latent_hbm, filter_hbm, mix_hbm, band_hbm, up_hbm, down_hbm, out_ref,
    latent_in, filter_in, mix_in, band_in, up_in, down_in,
    points, rows, parts_out, parts_in, back_out, back_in,
    gathered, ends, stack, table, mix_wide, mixer, turned, turned_last,
    load_sem, small_send_sem, mix_sem, band_sem, out_sem, side_sem, in_sem, back_send_sem, back_sem,
):
    lat, lon = lax.axis_index("lat"), lax.axis_index("lon")
    lats, lons = lax.axis_size("lat"), lax.axis_size("lon")
    width, _, channels = latent_in.shape
    count, length = filter_in.shape
    group = mix_in.shape[3]
    share = channels // WORKERS
    core = lax.rem(lat, 2)
    base = lat - core
    my_x, my_z = lon // Z_CHIPS, lax.rem(lon, Z_CHIPS)
    my_work = (my_x * WORK_Z + my_z) * 2 + core
    works = my_z < WORK_Z
    idle = jnp.logical_not(works)
    has_low, has_high = base > 0, base + 2 < lats
    aside = base + jnp.where(core == 0, -2, 2)
    has_side = jnp.where(core == 0, base > 0, base + 2 < lats)

    def load(source, target, n):
        return pltpu.make_async_copy(source, target, load_sem.at[n])

    latent_load = load(latent_hbm, latent_in, 0)
    filter_load = load(filter_hbm, filter_in, 1)
    band_load = load(band_hbm, band_in.at[core], 2)
    up_load = load(up_hbm, up_in, 3)
    down_load = load(down_hbm, down_in, 4)
    latent_load.start()

    def send(source, target, send_sem, recv_sem, device):
        return pltpu.make_async_remote_copy(
            src_ref=source,
            dst_ref=target,
            send_sem=send_sem,
            recv_sem=recv_sem,
            device_id=device,
            device_id_type=MESH,
        )

    barrier = pltpu.get_barrier_semaphore()

    def signal(to_lat, to_lon):
        pl.semaphore_signal(barrier, inc=1, device_id=(to_lat, to_lon), device_id_type=MESH)

    @pl.when(works)
    def _():
        for z in reversed(range(Z_CHIPS)):
            for x in range(X_CHIPS):
                to_lon = x * Z_CHIPS + z
                for c in range(2):
                    if z < WORK_Z:

                        @pl.when((lon != to_lon) | (core != c))
                        def _(c=c, to_lon=to_lon):
                            signal(base + c, to_lon)
                    else:
                        signal(base + c, to_lon)

        @pl.when(has_high)
        def _():
            for z in reversed(range(Z_CHIPS)):
                for x in range(X_CHIPS):
                    signal(base + 2, x * Z_CHIPS + z)

        @pl.when(has_low)
        def _():
            for z in reversed(range(Z_CHIPS)):
                for x in range(X_CHIPS):
                    signal(base - 1, x * Z_CHIPS + z)

    filter_load.start()
    band_load.start()

    pl.semaphore_wait(
        barrier,
        WORKERS - works.astype(jnp.int32) + jnp.where(has_side, WORKERS, 0),
    )

    mix_work = lon // 2
    mix_core = lax.rem(mix_work, 2)
    mix_lon = (mix_work // (2 * WORK_Z)) * Z_CHIPS + lax.rem(mix_work // 2, WORK_Z)
    half = lax.rem(lon, 2)
    mix_send = send(mix_hbm, mix_in.at[half], small_send_sem.at[0], mix_sem.at[half], (base + mix_core, mix_lon))
    mix_copy = pltpu.make_async_copy(mix_hbm, mix_in.at[half], mix_sem.at[half])
    band_send = send(band_hbm, band_in.at[core], small_send_sem.at[1], band_sem, (base + 1 - core, lon))
    mix_here = (core == mix_core) & (lon == mix_lon)
    mix_away = (core == 1) & jnp.logical_not(mix_here)

    @pl.when(works)
    def _():
        band_send.start()

    @pl.when(mix_away)
    def _():
        mix_send.start()

    @pl.when((core == 1) & mix_here)
    def _():
        mix_copy.start()

    blocks = channels // LANES
    columns = [slice(LANES * t, LANES * (t + 1)) for t in range(blocks)]
    rest = width - AHEAD
    places = [
        (slice(0, AHEAD), pl.ds(0, AHEAD, stride=2)),
        (slice(AHEAD, 2 * AHEAD), pl.ds(1, AHEAD, stride=2)),
        (slice(2 * AHEAD, 2 * AHEAD + rest), pl.ds(2 * AHEAD, rest, stride=2)),
        (slice(2 * AHEAD + rest, 2 * width), pl.ds(2 * AHEAD + 1, rest, stride=2)),
    ]
    latent_load.wait()
    for t, column in enumerate(columns):
        for n in range(width):
            points[t, 2 * n : 2 * n + 2, :] = latent_in[n, :, column].astype(F32)
        for place, point in places:
            rows[place, column] = points[t, point, :]

    lane = lax.broadcasted_iota(jnp.int32, (8, LANES), 1)
    upper = lax.broadcasted_iota(jnp.int32, (8, LANES), 0) < rest
    tiles = [rows[8 * q : 8 * q + 8, :] for q in range(3)]
    tiles[2] = jnp.where(lax.rem(lon, 2) == 1, pltpu.roll(tiles[2], rest, 0), tiles[2])
    for w in range(WORKERS):
        tile, place = divmod(w * share, LANES)
        message = jnp.zeros((8, LANES), F32)
        for q in range(3):
            piece = tiles[q][:, columns[tile]]
            if place + share > LANES:
                piece = jnp.where(lane >= place, piece, tiles[q][:, columns[tile + 1]])
            shift = (share * q - place) % LANES
            if shift:
                piece = pltpu.roll(piece, shift, 1)
            inside = (lane >= share * q) & (lane < share * (q + 1))
            message = jnp.where(inside, piece, message)
        parts_out[w] = message.astype(BF16)

    @pl.when(works)
    def _():
        parts_in[core + 1, lon] = parts_out[my_work]

    @pl.when(has_side)
    def _():
        slot = jnp.where(core == 0, 3, 0)
        for w, (c, to_lon) in enumerate(WORK_AT):
            send(parts_out.at[w], parts_in.at[slot, lon], side_sem, in_sem.at[slot], (aside + c, to_lon)).start()

    for w, (c, to_lon) in enumerate(WORK_AT):

        @pl.when((lon != to_lon) | (core != c))
        def _(w=w, c=c, to_lon=to_lon):
            send(parts_out.at[w], parts_in.at[core + 1, lon], out_sem, in_sem.at[core + 1], (base + c, to_lon)).start()

    up_load.start()
    down_load.start()
    filter_load.wait()
    band_load.wait()

    @pl.when(works)
    def _():
        row8 = lax.broadcasted_iota(jnp.int32, (8, length), 0)
        filters = filter_in[...].astype(F32)
        for k in range(count):
            first = jnp.broadcast_to(filters[k : k + 1, :], (8, length))
            first = pltpu.roll(first, 0, 1, stride=1, stride_axis=0)
            last = jnp.where(row8 < rest, pltpu.roll(first, AHEAD, 1), pltpu.roll(first, 2 * AHEAD, 1))
            first = jnp.concatenate([first, pltpu.roll(first, width, 1)], axis=0)
            last = jnp.concatenate([last, pltpu.roll(last, 2 * width, 1)], axis=0)
            top = k * length
            for p in range(lons // 2):
                turn = pltpu.roll(first, 2 * width * p, 1) if p else first
                table[top + 16 * p : top + 16 * p + 16, :] = turn.astype(BF16)
            top += 8 * lons
            for p in range(lons // 4):
                turn = pltpu.roll(last, 4 * width * p, 1) if p else last
                table[top + 16 * p : top + 16 * p + 16, :] = turn.astype(BF16)

        mix_wide[...] = jnp.zeros(mix_wide.shape, F32)
        for h in range(2):
            send(mix_hbm, mix_in.at[h], small_send_sem.at[0], mix_sem.at[h], (base, lon)).wait_recv()
        band_send.wait_recv()
        third = lax.broadcasted_iota(jnp.int32, (1, LANES), 1) // share
        lower = lax.broadcasted_iota(jnp.int32, (share, LANES), 0) >= group
        bands = [band_in[o].astype(F32) for o in range(2)]
        empty = jnp.zeros((share, LANES), F32)
        for k in range(count):
            for h in range(2):
                mix_wide[group * h : group * (h + 1), 0:group] = mix_in[h, k].astype(F32)
            once = mix_wide[...]
            once = jnp.where(lower, pltpu.roll(once, group, 1), once)
            every = once + pltpu.roll(once, share, 1) + pltpu.roll(once, 2 * share, 1)
            for o in range(2):
                scaled = []
                for i in range(2):
                    scale = jnp.zeros((1, LANES), F32)
                    for t in range(3):
                        scale = jnp.where(third == t, bands[o][t, i : i + 1, k : k + 1], scale)
                    scaled.append(every * scale)
                whole = jnp.concatenate(
                    [
                        jnp.concatenate([scaled[0], empty], axis=1),
                        jnp.concatenate([empty, scaled[1]], axis=1),
                    ],
                    axis=0,
                )
                mixer[o, 2 * share * k : 2 * share * (k + 1), :] = whole.astype(BF16)

        turned[:, length:, :] = jnp.zeros((2, turned.shape[1] - length, LANES), F32)

        def unfold(n):
            for b in range(lons):
                gathered[8 * b : 8 * b + 8, :] = parts_in[n, b].astype(F32)
            for p in range(lons // 2):
                even, odd = gathered[16 * p : 16 * p + 8, :], gathered[16 * p + 8 : 16 * p + 16, :]
                one = pltpu.roll(jnp.where(upper, odd, even), rest, 0)
                one = pltpu.roll(one, LANES - 2 * share, 1)
                ends[8 * p : 8 * p + 8, :] = jnp.where(lane >= 2 * share, jnp.where(upper, even, odd), one)
            first, last = gathered[...].T, ends[...].T
            top = 2 * share * n
            stack[top : top + 2 * share, 0 : 8 * lons] = first[0 : 2 * share]
            stack[top : top + share, 8 * lons :] = last[2 * share : 3 * share]
            stack[top + share : top + 2 * share, 8 * lons :] = last[0:share]

        def arrive(n, members):
            taken = parts_in.at[n, pl.ds(0, members)]
            send(taken, taken, out_sem, in_sem.at[n], (lat, 0)).wait_recv()

        for n, there in ((0, has_low), (3, has_high)):

            @pl.when(there)
            def _(n=n):
                arrive(n, lons)
                unfold(n)

            @pl.when(jnp.logical_not(there))
            def _(n=n):
                stack[2 * share * n : 2 * share * (n + 1), :] = jnp.zeros((2 * share, length), F32)

        for n in (1, 2):

            @pl.when(core + 1 == n)
            def _(n=n):
                arrive(n, lons - 1)

            @pl.when(core + 1 != n)
            def _(n=n):
                arrive(n, lons)

            unfold(n)

        pad = jnp.zeros((LANES - 3 * share, length), F32)
        sides = []
        for o in range(2):
            top = 2 * share * o
            wide = jnp.concatenate(
                [stack[top : top + 3 * share, :], pad, stack[top + 3 * share : top + 6 * share, :], pad], axis=0
            ).astype(BF16)
            mixed = jnp.dot(mixer[o], wide, preferred_element_type=F32).astype(BF16)
            sides.append(
                jnp.concatenate([mixed[2 * share * k : 2 * share * (k + 1), :] for k in range(count)], axis=1)
            )
        convolved = jnp.dot(jnp.concatenate(sides, axis=0), table[...], preferred_element_type=F32)

        for o in range(2):
            one = convolved[2 * share * o : 2 * share * (o + 1), :]
            one = jnp.concatenate([one, one[0:share], pad], axis=0).T
            turned[o, 0:length, :] = one
            turned_last[o] = pltpu.roll(one, share, 1)
        order = sorted(range(lons), key=lambda b: b % Z_CHIPS)
        for b in order:
            for o in (1, 0):
                start = turned[o, width * b : width * b + 8, :]
                end0 = turned[o, width * b + AHEAD : width * b + AHEAD + 8, :]
                end1 = turned_last[o, width * b + rest : width * b + rest + 8, :]
                message = jnp.where(lane < 2 * share, start, jnp.where(upper, end0, end1))
                back_out[o, b] = message.astype(BF16)
        back_in[my_work] = back_out[core, lon]
        for b in order:
            for o in (1, 0):
                back = send(back_out.at[o, b], back_in.at[my_work], back_send_sem.at[o], back_sem, (base + o, b))
                if b % Z_CHIPS < WORK_Z:

                    @pl.when((lon != b) | (core != o))
                    def _(back=back):
                        back.start()
                else:
                    back.start()

    def sent(buffer, members, sem):
        taken = buffer.at[pl.ds(0, members)]
        send(taken, taken, sem, back_sem, (lat, 0)).wait_send()

    def returned(members):
        taken = back_in.at[pl.ds(0, members)]
        send(taken, taken, out_sem, back_sem, (lat, 0)).wait_recv()

    up_load.wait()
    down_load.wait()

    @pl.when(works)
    def _():
        returned(WORKERS - 1)

    @pl.when(idle)
    def _():
        returned(WORKERS)

    sums = [[jnp.zeros((8, LANES), F32) for _ in range(blocks)] for _ in range(3)]
    for w in range(WORKERS):
        tile, place = divmod(w * share, LANES)
        message = back_in[w].astype(F32)
        for q in range(3):
            shift = (place - share * q) % LANES
            piece = pltpu.roll(message, shift, 1) if shift else message
            inside = (lane >= place) & (lane < place + share)
            sums[q][tile] = jnp.where(inside, piece, sums[q][tile])
            if place + share > LANES:
                sums[q][tile + 1] = jnp.where(lane < place + share - LANES, piece, sums[q][tile + 1])
    returned_rows = jnp.concatenate([jnp.concatenate(one, axis=1) for one in sums], axis=0)

    summed = (rows[...] + returned_rows).astype(BF16).astype(F32)
    mean = jnp.mean(summed, axis=1, keepdims=True)
    centred = summed - mean
    var = jnp.mean(centred * centred, axis=1, keepdims=True)
    normed = (centred * lax.rsqrt(var + 1e-05)).astype(BF16)
    hidden = erf_gelu(jnp.dot(normed, up_in[...], preferred_element_type=F32)).astype(BF16)
    result = summed + jnp.dot(hidden, down_in[...], preferred_element_type=F32)
    for t, column in enumerate(columns):
        for place, point in places:
            points[t, point, :] = result[place, column]
        for n in range(width):
            out_ref[n, :, column] = points[t, 2 * n : 2 * n + 2, :].astype(BF16)

    @pl.when(works)
    def _():
        sent(parts_out, WORKERS - 1, out_sem)
        for o in range(2):

            @pl.when(core == o)
            def _(o=o):
                sent(back_out.at[o], lons - 1, back_send_sem.at[o])

            @pl.when(core != o)
            def _(o=o):
                sent(back_out.at[o], lons, back_send_sem.at[o])

        band_send.wait_send()

    @pl.when(idle)
    def _():
        sent(parts_out, WORKERS, out_sem)

    @pl.when(has_side)
    def _():
        sent(parts_out, WORKERS, side_sem)

    @pl.when(mix_away)
    def _():
        mix_send.wait_send()


def local(latent, lon_filter, mix_weight, band_weight, offsets, w_up, w_down):
    del offsets
    latent, band_weight = jnp.transpose(latent, (1, 0, 2)), jnp.transpose(band_weight, (2, 1, 0))
    count, length = lon_filter.shape
    lons = lax.axis_size("lon")
    channels = w_up.shape[0]
    share = channels // WORKERS
    whole = pl.BlockSpec(memory_space=pl.ANY)
    result = pl.pallas_call(
        kernel,
        out_shape=jax.ShapeDtypeStruct(latent.shape, latent.dtype),
        in_specs=[whole] * 6,
        out_specs=pl.BlockSpec(memory_space=pltpu.VMEM),
        scratch_shapes=[
            pltpu.VMEM(latent.shape, BF16),
            pltpu.VMEM(lon_filter.shape, BF16),
            pltpu.VMEM((2, *mix_weight.shape), BF16),
            pltpu.VMEM((2, *band_weight.shape), BF16),
            pltpu.VMEM(w_up.shape, BF16),
            pltpu.VMEM(w_down.shape, BF16),
            pltpu.VMEM((channels // LANES, 2 * latent.shape[0], LANES), F32),
            pltpu.VMEM((2 * latent.shape[0], channels), F32),
            pltpu.VMEM((WORKERS, 8, LANES), BF16),
            pltpu.VMEM((4, lons, 8, LANES), BF16),
            pltpu.VMEM((2, lons, 8, LANES), BF16),
            pltpu.VMEM((WORKERS, 8, LANES), BF16),
            pltpu.VMEM((8 * lons, LANES), F32),
            pltpu.VMEM((4 * lons, LANES), F32),
            pltpu.VMEM((8 * share, length), F32),
            pltpu.VMEM((count * length, length), BF16),
            pltpu.VMEM((share, LANES), F32),
            pltpu.VMEM((2, count * 2 * share, 2 * LANES), BF16),
            pltpu.VMEM((2, length + 8, LANES), F32),
            pltpu.VMEM((2, length, LANES), F32),
            pltpu.SemaphoreType.DMA((5,)),
            pltpu.SemaphoreType.DMA((2,)),
            pltpu.SemaphoreType.DMA((2,)),
            pltpu.SemaphoreType.DMA,
            pltpu.SemaphoreType.DMA,
            pltpu.SemaphoreType.DMA,
            pltpu.SemaphoreType.DMA((4,)),
            pltpu.SemaphoreType.DMA((2,)),
            pltpu.SemaphoreType.DMA,
        ],
        compiler_params=pltpu.CompilerParams(collective_id=0, has_side_effects=True),
    )(latent, lon_filter, mix_weight, band_weight, w_up, w_down)
    return jnp.transpose(result, (1, 0, 2))


def solution(mesh):
    return jax.shard_map(
        local,
        mesh=mesh,
        in_specs=(
            P("lat", "lon", None),
            P(),
            P(None, "lon", None),
            P(None, "lat", None),
            P("lat"),
            P(),
            P(),
        ),
        out_specs=P("lat", "lon", None),
        check_vma=False,
    )
```

```python
import jax
import jax.numpy as jnp
from jax import lax
from jax.experimental import pallas as pl
from jax.experimental.pallas import tpu as pltpu
from jax.sharding import PartitionSpec as P

MESH = pl.DeviceIdType.MESH
F32 = jnp.float32
BF16 = jnp.bfloat16
X_CHIPS, Z_CHIPS = 4, 8
WORK_Z = 2
WORKERS = X_CHIPS * WORK_Z * 2
WORK_AT = [(core, x * Z_CHIPS + z) for x in range(X_CHIPS) for z in range(WORK_Z) for core in range(2)]
LANES = 128
AHEAD = 8


def erf_gelu(value):
    return 0.5 * value * (1.0 + lax.erf(value * 0.7071067811865476))


def kernel(
    latent_hbm, filter_hbm, mix_hbm, band_hbm, up_hbm, down_hbm, out_ref,
    latent_in, filter_in, mix_in, band_in, up_in, down_in,
    points, rows, parts_out, parts_in, back_out, back_in,
    gathered, ends, stack, table, mix_wide, mixer, turned, turned_last,
    load_sem, small_send_sem, mix_sem, band_sem, out_sem, side_sem, in_sem, back_send_sem, back_sem,
):
    lat, lon = lax.axis_index("lat"), lax.axis_index("lon")
    lats, lons = lax.axis_size("lat"), lax.axis_size("lon")
    width, _, channels = latent_in.shape
    count, length = filter_in.shape
    group = mix_in.shape[3]
    share = channels // WORKERS
    core = lax.rem(lat, 2)
    base = lat - core
    my_x, my_z = lon // Z_CHIPS, lax.rem(lon, Z_CHIPS)
    my_work = (my_x * WORK_Z + my_z) * 2 + core
    works = my_z < WORK_Z
    idle = jnp.logical_not(works)
    has_low, has_high = base > 0, base + 2 < lats
    aside = base + jnp.where(core == 0, -2, 2)
    has_side = jnp.where(core == 0, base > 0, base + 2 < lats)

    def load(source, target, n):
        return pltpu.make_async_copy(source, target, load_sem.at[n])

    latent_load = load(latent_hbm, latent_in, 0)
    filter_load = load(filter_hbm, filter_in, 1)
    band_load = load(band_hbm, band_in.at[core], 2)
    up_load = load(up_hbm, up_in, 3)
    down_load = load(down_hbm, down_in, 4)
    latent_load.start()

    def send(source, target, send_sem, recv_sem, device):
        return pltpu.make_async_remote_copy(
            src_ref=source,
            dst_ref=target,
            send_sem=send_sem,
            recv_sem=recv_sem,
            device_id=device,
            device_id_type=MESH,
        )

    barrier = pltpu.get_barrier_semaphore()

    def signal(to_lat, to_lon):
        pl.semaphore_signal(barrier, inc=1, device_id=(to_lat, to_lon), device_id_type=MESH)

    @pl.when(works)
    def _():
        for z in reversed(range(Z_CHIPS)):
            for x in range(X_CHIPS):
                to_lon = x * Z_CHIPS + z
                for c in range(2):
                    if z < WORK_Z:

                        @pl.when((lon != to_lon) | (core != c))
                        def _(c=c, to_lon=to_lon):
                            signal(base + c, to_lon)
                    else:
                        signal(base + c, to_lon)

        @pl.when(has_high)
        def _():
            for z in reversed(range(Z_CHIPS)):
                for x in range(X_CHIPS):
                    signal(base + 2, x * Z_CHIPS + z)

        @pl.when(has_low)
        def _():
            for z in reversed(range(Z_CHIPS)):
                for x in range(X_CHIPS):
                    signal(base - 1, x * Z_CHIPS + z)

    filter_load.start()
    band_load.start()

    pl.semaphore_wait(
        barrier,
        WORKERS - works.astype(jnp.int32) + jnp.where(has_side, WORKERS, 0),
    )

    mix_work = lon // 2
    mix_core = lax.rem(mix_work, 2)
    mix_lon = (mix_work // (2 * WORK_Z)) * Z_CHIPS + lax.rem(mix_work // 2, WORK_Z)
    half = lax.rem(lon, 2)
    mix_send = send(mix_hbm, mix_in.at[half], small_send_sem.at[0], mix_sem.at[half], (base + mix_core, mix_lon))
    mix_copy = pltpu.make_async_copy(mix_hbm, mix_in.at[half], mix_sem.at[half])
    band_send = send(band_hbm, band_in.at[core], small_send_sem.at[1], band_sem, (base + 1 - core, lon))
    mix_here = (core == mix_core) & (lon == mix_lon)
    mix_away = (core == 1) & jnp.logical_not(mix_here)

    @pl.when(works)
    def _():
        band_send.start()

    @pl.when(mix_away)
    def _():
        mix_send.start()

    @pl.when((core == 1) & mix_here)
    def _():
        mix_copy.start()

    blocks = channels // LANES
    columns = [slice(LANES * t, LANES * (t + 1)) for t in range(blocks)]
    rest = width - AHEAD
    places = [
        (slice(0, AHEAD), pl.ds(0, AHEAD, stride=2)),
        (slice(AHEAD, 2 * AHEAD), pl.ds(1, AHEAD, stride=2)),
        (slice(2 * AHEAD, 2 * AHEAD + rest), pl.ds(2 * AHEAD, rest, stride=2)),
        (slice(2 * AHEAD + rest, 2 * width), pl.ds(2 * AHEAD + 1, rest, stride=2)),
    ]
    latent_load.wait()
    for t, column in enumerate(columns):
        for n in range(width):
            points[t, 2 * n : 2 * n + 2, :] = latent_in[n, :, column].astype(F32)
        for place, point in places:
            rows[place, column] = points[t, point, :]

    lane = lax.broadcasted_iota(jnp.int32, (8, LANES), 1)
    upper = lax.broadcasted_iota(jnp.int32, (8, LANES), 0) < rest
    tiles = [rows[8 * q : 8 * q + 8, :] for q in range(3)]
    tiles[2] = jnp.where(lax.rem(lon, 2) == 1, pltpu.roll(tiles[2], rest, 0), tiles[2])
    for w in range(WORKERS):
        tile, place = divmod(w * share, LANES)
        message = jnp.zeros((8, LANES), F32)
        for q in range(3):
            piece = tiles[q][:, columns[tile]]
            if place + share > LANES:
                piece = jnp.where(lane >= place, piece, tiles[q][:, columns[tile + 1]])
            shift = (share * q - place) % LANES
            if shift:
                piece = pltpu.roll(piece, shift, 1)
            inside = (lane >= share * q) & (lane < share * (q + 1))
            message = jnp.where(inside, piece, message)
        parts_out[w] = message.astype(BF16)

    @pl.when(works)
    def _():
        parts_in[core + 1, lon] = parts_out[my_work]

    @pl.when(has_side)
    def _():
        slot = jnp.where(core == 0, 3, 0)
        for w, (c, to_lon) in enumerate(WORK_AT):
            send(parts_out.at[w], parts_in.at[slot, lon], side_sem, in_sem.at[slot], (aside + c, to_lon)).start()

    for w, (c, to_lon) in enumerate(WORK_AT):

        @pl.when((lon != to_lon) | (core != c))
        def _(w=w, c=c, to_lon=to_lon):
            send(parts_out.at[w], parts_in.at[core + 1, lon], out_sem, in_sem.at[core + 1], (base + c, to_lon)).start()

    up_load.start()
    down_load.start()
    filter_load.wait()
    band_load.wait()

    @pl.when(works)
    def _():
        row8 = lax.broadcasted_iota(jnp.int32, (8, length), 0)
        filters = filter_in[...].astype(F32)
        for k in range(count):
            first = jnp.broadcast_to(filters[k : k + 1, :], (8, length))
            first = pltpu.roll(first, 0, 1, stride=1, stride_axis=0)
            last = jnp.where(row8 < rest, pltpu.roll(first, AHEAD, 1), pltpu.roll(first, 2 * AHEAD, 1))
            first = jnp.concatenate([first, pltpu.roll(first, width, 1)], axis=0)
            last = jnp.concatenate([last, pltpu.roll(last, 2 * width, 1)], axis=0)
            top = k * length
            for p in range(lons // 2):
                turn = pltpu.roll(first, 2 * width * p, 1) if p else first
                table[top + 16 * p : top + 16 * p + 16, :] = turn.astype(BF16)
            top += 8 * lons
            for p in range(lons // 4):
                turn = pltpu.roll(last, 4 * width * p, 1) if p else last
                table[top + 16 * p : top + 16 * p + 16, :] = turn.astype(BF16)

        mix_wide[...] = jnp.zeros(mix_wide.shape, F32)
        for h in range(2):
            send(mix_hbm, mix_in.at[h], small_send_sem.at[0], mix_sem.at[h], (base, lon)).wait_recv()
        band_send.wait_recv()
        third = lax.broadcasted_iota(jnp.int32, (1, LANES), 1) // share
        lower = lax.broadcasted_iota(jnp.int32, (share, LANES), 0) >= group
        bands = [band_in[o].astype(F32) for o in range(2)]
        empty = jnp.zeros((share, LANES), F32)
        for k in range(count):
            for h in range(2):
                mix_wide[group * h : group * (h + 1), 0:group] = mix_in[h, k].astype(F32)
            once = mix_wide[...]
            once = jnp.where(lower, pltpu.roll(once, group, 1), once)
            every = once + pltpu.roll(once, share, 1) + pltpu.roll(once, 2 * share, 1)
            for o in range(2):
                scaled = []
                for i in range(2):
                    scale = jnp.zeros((1, LANES), F32)
                    for t in range(3):
                        scale = jnp.where(third == t, bands[o][t, i : i + 1, k : k + 1], scale)
                    scaled.append(every * scale)
                whole = jnp.concatenate(
                    [
                        jnp.concatenate([scaled[0], empty], axis=1),
                        jnp.concatenate([empty, scaled[1]], axis=1),
                    ],
                    axis=0,
                )
                mixer[o, 2 * share * k : 2 * share * (k + 1), :] = whole.astype(BF16)

        turned[:, length:, :] = jnp.zeros((2, turned.shape[1] - length, LANES), F32)

        def unfold(n):
            for b in range(lons):
                gathered[8 * b : 8 * b + 8, :] = parts_in[n, b].astype(F32)
            for p in range(lons // 2):
                even, odd = gathered[16 * p : 16 * p + 8, :], gathered[16 * p + 8 : 16 * p + 16, :]
                one = pltpu.roll(jnp.where(upper, odd, even), rest, 0)
                one = pltpu.roll(one, LANES - 2 * share, 1)
                ends[8 * p : 8 * p + 8, :] = jnp.where(lane >= 2 * share, jnp.where(upper, even, odd), one)
            first, last = gathered[...].T, ends[...].T
            top = 2 * share * n
            stack[top : top + 2 * share, 0 : 8 * lons] = first[0 : 2 * share]
            stack[top : top + share, 8 * lons :] = last[2 * share : 3 * share]
            stack[top + share : top + 2 * share, 8 * lons :] = last[0:share]

        def arrive(n, members):
            taken = parts_in.at[n, pl.ds(0, members)]
            send(taken, taken, out_sem, in_sem.at[n], (lat, 0)).wait_recv()

        for n, there in ((0, has_low), (3, has_high)):

            @pl.when(there)
            def _(n=n):
                arrive(n, lons)
                unfold(n)

            @pl.when(jnp.logical_not(there))
            def _(n=n):
                stack[2 * share * n : 2 * share * (n + 1), :] = jnp.zeros((2 * share, length), F32)

        for n in (1, 2):

            @pl.when(core + 1 == n)
            def _(n=n):
                arrive(n, lons - 1)

            @pl.when(core + 1 != n)
            def _(n=n):
                arrive(n, lons)

            unfold(n)

        pad = jnp.zeros((LANES - 3 * share, length), F32)
        sides = []
        for o in range(2):
            top = 2 * share * o
            wide = jnp.concatenate(
                [stack[top : top + 3 * share, :], pad, stack[top + 3 * share : top + 6 * share, :], pad], axis=0
            ).astype(BF16)
            mixed = jnp.dot(mixer[o], wide, preferred_element_type=F32).astype(BF16)
            sides.append(
                jnp.concatenate([mixed[2 * share * k : 2 * share * (k + 1), :] for k in range(count)], axis=1)
            )
        convolved = jnp.dot(jnp.concatenate(sides, axis=0), table[...], preferred_element_type=F32)

        for o in range(2):
            one = convolved[2 * share * o : 2 * share * (o + 1), :]
            one = jnp.concatenate([one, one[0:share], pad], axis=0).T
            turned[o, 0:length, :] = one
            turned_last[o] = pltpu.roll(one, share, 1)
        order = sorted(range(lons), key=lambda b: b % Z_CHIPS)
        for b in order:
            for o in (1, 0):
                start = turned[o, width * b : width * b + 8, :]
                end0 = turned[o, width * b + AHEAD : width * b + AHEAD + 8, :]
                end1 = turned_last[o, width * b + rest : width * b + rest + 8, :]
                message = jnp.where(lane < 2 * share, start, jnp.where(upper, end0, end1))
                back_out[o, b] = message.astype(BF16)
        back_in[my_work] = back_out[core, lon]
        for b in order:
            for o in (1, 0):
                back = send(back_out.at[o, b], back_in.at[my_work], back_send_sem.at[o], back_sem, (base + o, b))
                if b % Z_CHIPS < WORK_Z:

                    @pl.when((lon != b) | (core != o))
                    def _(back=back):
                        back.start()
                else:
                    back.start()

    def sent(buffer, members, sem):
        taken = buffer.at[pl.ds(0, members)]
        send(taken, taken, sem, back_sem, (lat, 0)).wait_send()

    def returned(members):
        taken = back_in.at[pl.ds(0, members)]
        send(taken, taken, out_sem, back_sem, (lat, 0)).wait_recv()

    up_load.wait()
    down_load.wait()

    @pl.when(works)
    def _():
        returned(WORKERS - 1)

    @pl.when(idle)
    def _():
        returned(WORKERS)

    sums = [[jnp.zeros((8, LANES), F32) for _ in range(blocks)] for _ in range(3)]
    for w in range(WORKERS):
        tile, place = divmod(w * share, LANES)
        message = back_in[w].astype(F32)
        for q in range(3):
            shift = (place - share * q) % LANES
            piece = pltpu.roll(message, shift, 1) if shift else message
            inside = (lane >= place) & (lane < place + share)
            sums[q][tile] = jnp.where(inside, piece, sums[q][tile])
            if place + share > LANES:
                sums[q][tile + 1] = jnp.where(lane < place + share - LANES, piece, sums[q][tile + 1])
    returned_rows = jnp.concatenate([jnp.concatenate(one, axis=1) for one in sums], axis=0)

    summed = (rows[...] + returned_rows).astype(BF16).astype(F32)
    mean = jnp.mean(summed, axis=1, keepdims=True)
    centred = summed - mean
    var = jnp.mean(centred * centred, axis=1, keepdims=True)
    normed = (centred * lax.rsqrt(var + 1e-05)).astype(BF16)
    hidden = erf_gelu(jnp.dot(normed, up_in[...], preferred_element_type=F32)).astype(BF16)
    result = summed + jnp.dot(hidden, down_in[...], preferred_element_type=F32)
    for t, column in enumerate(columns):
        for place, point in places:
            points[t, point, :] = result[place, column]
        for n in range(width):
            out_ref[n, :, column] = points[t, 2 * n : 2 * n + 2, :].astype(BF16)

    @pl.when(works)
    def _():
        sent(parts_out, WORKERS - 1, out_sem)
        for o in range(2):

            @pl.when(core == o)
            def _(o=o):
                sent(back_out.at[o], lons - 1, back_send_sem.at[o])

            @pl.when(core != o)
            def _(o=o):
                sent(back_out.at[o], lons, back_send_sem.at[o])

        band_send.wait_send()

    @pl.when(idle)
    def _():
        sent(parts_out, WORKERS, out_sem)

    @pl.when(has_side)
    def _():
        sent(parts_out, WORKERS, side_sem)

    @pl.when(mix_away)
    def _():
        mix_send.wait_send()


def local(latent, lon_filter, mix_weight, band_weight, offsets, w_up, w_down):
    del offsets
    latent, band_weight = jnp.transpose(latent, (1, 0, 2)), jnp.transpose(band_weight, (2, 1, 0))
    count, length = lon_filter.shape
    lons = lax.axis_size("lon")
    channels = w_up.shape[0]
    share = channels // WORKERS
    whole = pl.BlockSpec(memory_space=pltpu.HBM)
    result = pl.pallas_call(
        kernel,
        out_shape=jax.ShapeDtypeStruct(latent.shape, latent.dtype),
        in_specs=[whole] * 6,
        out_specs=pl.BlockSpec(memory_space=pltpu.VMEM),
        scratch_shapes=[
            pltpu.VMEM(latent.shape, BF16),
            pltpu.VMEM(lon_filter.shape, BF16),
            pltpu.VMEM((2, *mix_weight.shape), BF16),
            pltpu.VMEM((2, *band_weight.shape), BF16),
            pltpu.VMEM(w_up.shape, BF16),
            pltpu.VMEM(w_down.shape, BF16),
            pltpu.VMEM((channels // LANES, 2 * latent.shape[0], LANES), F32),
            pltpu.VMEM((2 * latent.shape[0], channels), F32),
            pltpu.VMEM((WORKERS, 8, LANES), BF16),
            pltpu.VMEM((4, lons, 8, LANES), BF16),
            pltpu.VMEM((2, lons, 8, LANES), BF16),
            pltpu.VMEM((WORKERS, 8, LANES), BF16),
            pltpu.VMEM((8 * lons, LANES), F32),
            pltpu.VMEM((4 * lons, LANES), F32),
            pltpu.VMEM((8 * share, length), F32),
            pltpu.VMEM((count * length, length), BF16),
            pltpu.VMEM((share, LANES), F32),
            pltpu.VMEM((2, count * 2 * share, 2 * LANES), BF16),
            pltpu.VMEM((2, length + 8, LANES), F32),
            pltpu.VMEM((2, length, LANES), F32),
            pltpu.SemaphoreType.DMA((5,)),
            pltpu.SemaphoreType.DMA((2,)),
            pltpu.SemaphoreType.DMA((2,)),
            pltpu.SemaphoreType.DMA,
            pltpu.SemaphoreType.DMA,
            pltpu.SemaphoreType.DMA,
            pltpu.SemaphoreType.DMA((4,)),
            pltpu.SemaphoreType.DMA((2,)),
            pltpu.SemaphoreType.DMA,
        ],
        compiler_params=pltpu.CompilerParams(vmem_limit_bytes=16384 << 10, collective_id=0, has_side_effects=True),
    )(*(pltpu.with_memory_space_constraint(x, pltpu.HBM) for x in (latent, lon_filter, mix_weight, band_weight, w_up, w_down)))
    return jnp.transpose(result, (1, 0, 2))


def solution(mesh):
    return jax.shard_map(
        local,
        mesh=mesh,
        in_specs=(
            P("lat", "lon", None),
            P(),
            P(None, "lon", None),
            P(None, "lat", None),
            P("lat"),
            P(),
            P(),
        ),
        out_specs=P("lat", "lon", None),
        check_vma=False,
    )
```

```python
import jax
import jax.numpy as jnp
from jax import lax
from jax.experimental import pallas as pl
from jax.experimental.pallas import tpu as pltpu
from jax.sharding import PartitionSpec as P

MESH = pl.DeviceIdType.MESH
F32 = jnp.float32
BF16 = jnp.bfloat16
X_CHIPS, Z_CHIPS = 4, 8
WORK_Z = 2
WORKERS = X_CHIPS * WORK_Z * 2
WORK_AT = [(core, x * Z_CHIPS + z) for x in range(X_CHIPS) for z in range(WORK_Z) for core in range(2)]
LANES = 128
AHEAD = 8
GROUPS = 2
WIDE = 2 * LANES
PACK, PACK_ROWS = 6, 32


def erf_gelu(value):
    return 0.5 * value * (1.0 + lax.erf(value * 0.7071067811865476))


def kernel(
    latent_hbm, filter_hbm, mix_hbm, band_hbm, up_hbm, down_hbm, out_ref,
    latent_in, filter_in, mix_in, band_in, up_in, down_in,
    points, rows, mix_own, mix_out, parts_out, parts_in, back_out, back_in,
    gathered, stack, plain, table, mix_wide, mixer, total, turned, turned_last,
    load_sem, small_send_sem, mix_sem, band_sem, out_sem, side_sem, in_sem, back_send_sem, back_sem,
):
    lat, lon = lax.axis_index("lat"), lax.axis_index("lon")
    lats, lons = lax.axis_size("lat"), lax.axis_size("lon")
    width, _, channels = latent_in.shape
    count, length = filter_in.shape
    group = mix_own.shape[1]
    members = lons // GROUPS
    my_x, my_z = lon // Z_CHIPS, lax.rem(lon, Z_CHIPS)
    my_place = my_z * X_CHIPS + my_x
    my_group = my_place // members
    share = channels // WORKERS
    core = lax.rem(lat, 2)
    base = lat - core
    my_work = (my_x * WORK_Z + my_z) * 2 + core
    works = my_z < WORK_Z
    idle = jnp.logical_not(works)
    has_low, has_high = base > 0, base + 2 < lats
    aside = base + jnp.where(core == 0, -2, 2)
    has_side = jnp.where(core == 0, base > 0, base + 2 < lats)

    def load(source, target, n):
        return pltpu.make_async_copy(source, target, load_sem.at[n])

    latent_load = load(latent_hbm, latent_in, 0)
    filter_load = load(filter_hbm, filter_in, 1)
    band_load = load(band_hbm, band_in.at[core], 2)
    up_load = load(up_hbm, up_in, 3)
    down_load = load(down_hbm, down_in, 4)
    mix_load = load(mix_hbm, mix_own, 5)
    latent_load.start()

    @pl.when(core == 1)
    def _():
        mix_load.start()


    def send(source, target, send_sem, recv_sem, device):
        return pltpu.make_async_remote_copy(
            src_ref=source,
            dst_ref=target,
            send_sem=send_sem,
            recv_sem=recv_sem,
            device_id=device,
            device_id_type=MESH,
        )

    barrier = pltpu.get_barrier_semaphore()

    def signal(to_lat, to_lon):
        pl.semaphore_signal(barrier, inc=1, device_id=(to_lat, to_lon), device_id_type=MESH)

    @pl.when(works)
    def _():
        for z in reversed(range(Z_CHIPS)):
            for x in range(X_CHIPS):
                to_lon = x * Z_CHIPS + z
                for c in range(2):
                    if z < WORK_Z:

                        @pl.when((lon != to_lon) | (core != c))
                        def _(c=c, to_lon=to_lon):
                            signal(base + c, to_lon)
                    else:
                        signal(base + c, to_lon)

        @pl.when(has_high)
        def _():
            for z in reversed(range(Z_CHIPS)):
                for x in range(X_CHIPS):
                    signal(base + 2, x * Z_CHIPS + z)

        @pl.when(has_low)
        def _():
            for z in reversed(range(Z_CHIPS)):
                for x in range(X_CHIPS):
                    signal(base - 1, x * Z_CHIPS + z)

    filter_load.start()
    band_load.start()

    pl.semaphore_wait(
        barrier,
        WORKERS - works.astype(jnp.int32) + jnp.where(has_side, WORKERS, 0),
    )

    mix_work = lon // 2
    mix_core = lax.rem(mix_work, 2)
    mix_lon = (mix_work // (2 * WORK_Z)) * Z_CHIPS + lax.rem(mix_work // 2, WORK_Z)
    half = lax.rem(lon, 2)
    mix_send = send(mix_out, mix_in.at[half], small_send_sem.at[0], mix_sem.at[half], (base + mix_core, mix_lon))
    mix_copy = pltpu.make_async_copy(mix_out, mix_in.at[half], mix_sem.at[half])
    band_send = send(band_hbm, band_in.at[core], small_send_sem.at[1], band_sem, (base + 1 - core, lon))
    mix_here = (core == mix_core) & (lon == mix_lon)
    mix_away = (core == 1) & jnp.logical_not(mix_here)

    @pl.when(works)
    def _():
        band_send.start()

    blocks = channels // LANES
    columns = [slice(LANES * t, LANES * (t + 1)) for t in range(blocks)]
    rest = width - AHEAD
    places = [
        (slice(0, AHEAD), pl.ds(0, AHEAD, stride=2)),
        (slice(AHEAD, 2 * AHEAD), pl.ds(1, AHEAD, stride=2)),
        (slice(2 * AHEAD, 2 * AHEAD + rest), pl.ds(2 * AHEAD, rest, stride=2)),
        (slice(2 * AHEAD + rest, 2 * width), pl.ds(2 * AHEAD + 1, rest, stride=2)),
    ]
    latent_load.wait()
    for t, column in enumerate(columns):
        for n in range(width):
            points[t, 2 * n : 2 * n + 2, :] = latent_in[n, :, column].astype(F32)
        for place, point in places:
            rows[place, column] = points[t, point, :]

    lane = lax.broadcasted_iota(jnp.int32, (8, LANES), 1)
    upper = lax.broadcasted_iota(jnp.int32, (8, LANES), 0) < rest
    tiles = [rows[8 * q : 8 * q + 8, :] for q in range(3)]
    tiles[2] = jnp.where(lax.rem(my_x, 2) == 1, pltpu.roll(tiles[2], rest, 0), tiles[2])
    for w in range(WORKERS):
        tile, place = divmod(w * share, LANES)
        message = jnp.zeros((8, LANES), F32)
        for q in range(3):
            piece = tiles[q][:, columns[tile]]
            if place + share > LANES:
                piece = jnp.where(lane >= place, piece, tiles[q][:, columns[tile + 1]])
            shift = (share * q - place) % LANES
            if shift:
                piece = pltpu.roll(piece, shift, 1)
            inside = (lane >= share * q) & (lane < share * (q + 1))
            message = jnp.where(inside, piece, message)
        parts_out[w] = message.astype(BF16)

    @pl.when(works)
    def _():
        parts_in[core + 1, my_place] = parts_out[my_work]

    @pl.when(has_side)
    def _():
        slot = jnp.where(core == 0, 3, 0)
        for w, (c, to_lon) in enumerate(WORK_AT):
            send(parts_out.at[w], parts_in.at[slot, my_place], side_sem, in_sem.at[slot, my_group], (aside + c, to_lon)).start()

    @pl.when(core == 1)
    def _():
        mix_load.wait()
        mix_wide[...] = jnp.zeros(mix_wide.shape, F32)
        for first in range(0, count, PACK):
            packed = jnp.zeros((share, LANES), F32)
            for n in range(min(PACK, count - first)):
                mix_wide[0:group, 0:group] = mix_own[first + n].astype(F32)
                packed = packed + (pltpu.roll(mix_wide[...], group * n, 1) if n else mix_wide[...])
            mix_out[first // PACK] = packed[0:PACK_ROWS].astype(BF16)

    @pl.when(mix_away)
    def _():
        mix_send.start()

    @pl.when((core == 1) & mix_here)
    def _():
        mix_copy.start()

    for w, (c, to_lon) in enumerate(WORK_AT):

        @pl.when((lon != to_lon) | (core != c))
        def _(w=w, c=c, to_lon=to_lon):
            send(
                parts_out.at[w], parts_in.at[core + 1, my_place], out_sem, in_sem.at[core + 1, my_group], (base + c, to_lon)
            ).start()

    up_load.start()
    down_load.start()
    filter_load.wait()
    band_load.wait()

    @pl.when(works)
    def _():
        row8 = lax.broadcasted_iota(jnp.int32, (8, length), 0)
        column_of = lax.broadcasted_iota(jnp.int32, (length, length), 1)
        chip_z, chip_x = column_of // (X_CHIPS * width), lax.rem(column_of // width, X_CHIPS)
        column_of = (chip_x * Z_CHIPS + chip_z) * width + lax.rem(column_of, width)
        order = (column_of == lax.broadcasted_iota(jnp.int32, (length, length), 0)).astype(F32).astype(BF16)
        for g in range(GROUPS):
            plain[WIDE * g + 12 * members : WIDE * (g + 1), :] = jnp.zeros((WIDE - 12 * members, length), BF16)
        filters = filter_in[...].astype(F32)
        for k in range(count):
            first = jnp.broadcast_to(filters[k : k + 1, :], (8, length))
            first = pltpu.roll(first, 0, 1, stride=1, stride_axis=0)
            step = Z_CHIPS * width
            last = jnp.where(row8 < rest, pltpu.roll(first, AHEAD, 1), pltpu.roll(first, AHEAD + step - rest, 1))
            first = jnp.concatenate([first, pltpu.roll(first, step, 1)], axis=0)
            last = jnp.concatenate([last, pltpu.roll(last, 2 * step, 1)], axis=0)
            for z in range(Z_CHIPS):
                g, at = divmod(z * X_CHIPS, members)
                for x in range(0, X_CHIPS, 2):
                    shift = (x * step + z * width) % length
                    turn = pltpu.roll(first, shift, 1) if shift else first
                    row = WIDE * g + 8 * (at + x)
                    plain[row : row + 16, :] = turn.astype(BF16)
                turn = pltpu.roll(last, z * width, 1) if z else last
                row = WIDE * g + 8 * members + 4 * at
                plain[row : row + 16, :] = turn.astype(BF16)
            for g in range(GROUPS):
                top = (g * count + k) * WIDE
                table[top : top + WIDE, :] = jnp.dot(
                    plain[WIDE * g : WIDE * (g + 1), :], order, preferred_element_type=F32
                ).astype(BF16)

        gathered[:, 12 * members :, :] = jnp.zeros((4, WIDE - 12 * members, LANES), F32)

        @pl.when(jnp.logical_not(has_low))
        def _():
            parts_in[0] = jnp.zeros(parts_in.shape[1:], BF16)

        @pl.when(jnp.logical_not(has_high))
        def _():
            parts_in[3] = jnp.zeros(parts_in.shape[1:], BF16)

        def arrive(n, g, some):
            taken = parts_in.at[n, pl.ds(0, some)]
            send(taken, taken, out_sem, in_sem.at[n, g], (base, lon)).wait_recv()

        def unfold(n, g):
            for p in range(members // 2):
                even, odd = (parts_in[n, g * members + 2 * p + m].astype(F32) for m in range(2))
                gathered[n, 16 * p : 16 * p + 8, :] = even
                gathered[n, 16 * p + 8 : 16 * p + 16, :] = odd
                one = pltpu.roll(jnp.where(upper, odd, even), rest, 0)
                one = pltpu.roll(one, LANES - share, 1)
                zero = pltpu.roll(jnp.where(upper, even, odd), LANES - 2 * share, 1)
                row = 8 * members + 8 * p
                gathered[n, row : row + 8, :] = jnp.where(lane < share, zero, one)
            stack[2 * share * n : 2 * share * (n + 1), WIDE * g : WIDE * (g + 1)] = gathered[n].T[0 : 2 * share]

        def take(g):
            for n, there in ((0, has_low), (3, has_high)):

                @pl.when(there)
                def _(n=n):
                    arrive(n, g, members)

            for n in (1, 2):
                if g * members < WORK_Z * X_CHIPS:
                    own = (core + 1 == n) & (my_group == g)

                    @pl.when(own)
                    def _(n=n):
                        arrive(n, g, members - 1)

                    @pl.when(jnp.logical_not(own))
                    def _(n=n):
                        arrive(n, g, members)
                else:
                    arrive(n, g, members)
            for n in range(4):
                unfold(n, g)

        def mix(g):
            pad = jnp.zeros((LANES - 3 * share, WIDE), F32)
            lanes = slice(WIDE * g, WIDE * (g + 1))
            sides = []
            for o in range(2):
                top = 2 * share * o
                wide = jnp.concatenate(
                    [stack[top : top + 3 * share, lanes], pad, stack[top + 3 * share : top + 6 * share, lanes], pad],
                    axis=0,
                ).astype(BF16)
                mixed = jnp.dot(mixer[o], wide, preferred_element_type=F32).astype(BF16)
                sides.append(
                    jnp.concatenate([mixed[2 * share * k : 2 * share * (k + 1), :] for k in range(count)], axis=1)
                )
            return jnp.concatenate(sides, axis=0)

        def part(g, start, end):
            return table[count * WIDE * g : count * WIDE * (g + 1), start:end]

        take(0)

        for h in range(2):
            send(mix_out, mix_in.at[h], small_send_sem.at[0], mix_sem.at[h], (base, lon)).wait_recv()
        band_send.wait_recv()
        third = lax.broadcasted_iota(jnp.int32, (1, LANES), 1) // share
        wide_lane = lax.broadcasted_iota(jnp.int32, (PACK_ROWS, LANES), 1)
        bands = [band_in[o].astype(F32) for o in range(2)]
        empty = jnp.zeros((share, LANES), F32)
        for k in range(count):
            for h in range(2):
                shift = (group * h - group * (k % PACK)) % LANES
                once = mix_in[h, k // PACK].astype(F32)
                once = pltpu.roll(once, shift, 1) if shift else once
                once = jnp.where((wide_lane >= group * h) & (wide_lane < group * (h + 1)), once, 0.0)
                mix_wide[group * h : group * (h + 1), :] = once[0:group]
            once = mix_wide[...]
            every = once + pltpu.roll(once, share, 1) + pltpu.roll(once, 2 * share, 1)
            for o in range(2):
                scaled = []
                for i in range(2):
                    scale = jnp.zeros((1, LANES), F32)
                    for t in range(3):
                        scale = jnp.where(third == t, bands[o][t, i : i + 1, k : k + 1], scale)
                    scaled.append(every * scale)
                whole = jnp.concatenate(
                    [
                        jnp.concatenate([scaled[0], empty], axis=1),
                        jnp.concatenate([empty, scaled[1]], axis=1),
                    ],
                    axis=0,
                )
                mixer[o, 2 * share * k : 2 * share * (k + 1), :] = whole.astype(BF16)

        total[...] = jnp.dot(mix(0), part(0, 0, length), preferred_element_type=F32)
        turned[:, length:, :] = jnp.zeros((2, turned.shape[1] - length, LANES), F32)
        take(1)
        late = mix(1)

        def finish(start, end, chips):
            convolved = total[:, start:end] + jnp.dot(late, part(1, start, end), preferred_element_type=F32)
            fill = jnp.zeros((LANES - 3 * share, end - start), F32)
            for o in range(2):
                one = convolved[2 * share * o : 2 * share * (o + 1), :]
                one = jnp.concatenate([one, one[0:share], fill], axis=0).T
                turned[o, start:end, :] = one
                turned_last[o, start:end, :] = pltpu.roll(one, share, 1)
            for z in chips:
                for x in range(X_CHIPS):
                    b, at = x * Z_CHIPS + z, (z * X_CHIPS + x) * width
                    for o in range(2):
                        begin = turned[o, at : at + 8, :]
                        end0 = turned[o, at + AHEAD : at + AHEAD + 8, :]
                        end1 = turned_last[o, at + rest : at + rest + 8, :]
                        message = jnp.where(lane < 2 * share, begin, jnp.where(upper, end0, end1))
                        back_out[o, b] = message.astype(BF16)
            for z in chips:
                for x in range(X_CHIPS):
                    b = x * Z_CHIPS + z
                    for o in range(2):
                        back = send(back_out.at[o, b], back_in.at[my_work], back_send_sem.at[o], back_sem, (base + o, b))
                        if z < WORK_Z:

                            @pl.when((lon != b) | (core != o))
                            def _(back=back):
                                back.start()
                        else:
                            back.start()

        finish(0, LANES, range(WORK_Z))
        back_in[my_work] = back_out[core, lon]
        finish(LANES, length, range(WORK_Z, Z_CHIPS))

    def sent(buffer, members, sem):
        taken = buffer.at[pl.ds(0, members)]
        send(taken, taken, sem, back_sem, (lat, 0)).wait_send()

    def returned(members):
        taken = back_in.at[pl.ds(0, members)]
        send(taken, taken, out_sem, back_sem, (lat, 0)).wait_recv()

    up_load.wait()
    down_load.wait()

    @pl.when(works)
    def _():
        returned(WORKERS - 1)

    @pl.when(idle)
    def _():
        returned(WORKERS)

    sums = [[jnp.zeros((8, LANES), F32) for _ in range(blocks)] for _ in range(3)]
    for w in range(WORKERS):
        tile, place = divmod(w * share, LANES)
        message = back_in[w].astype(F32)
        for q in range(3):
            shift = (place - share * q) % LANES
            piece = pltpu.roll(message, shift, 1) if shift else message
            inside = (lane >= place) & (lane < place + share)
            sums[q][tile] = jnp.where(inside, piece, sums[q][tile])
            if place + share > LANES:
                sums[q][tile + 1] = jnp.where(lane < place + share - LANES, piece, sums[q][tile + 1])
    returned_rows = jnp.concatenate([jnp.concatenate(one, axis=1) for one in sums], axis=0)

    summed = (rows[...] + returned_rows).astype(BF16).astype(F32)
    mean = jnp.mean(summed, axis=1, keepdims=True)
    centred = summed - mean
    var = jnp.mean(centred * centred, axis=1, keepdims=True)
    normed = (centred * lax.rsqrt(var + 1e-05)).astype(BF16)
    hidden = erf_gelu(jnp.dot(normed, up_in[...], preferred_element_type=F32)).astype(BF16)
    result = summed + jnp.dot(hidden, down_in[...], preferred_element_type=F32)
    for t, column in enumerate(columns):
        for place, point in places:
            points[t, point, :] = result[place, column]
        for n in range(width):
            out_ref[n, :, column] = points[t, 2 * n : 2 * n + 2, :].astype(BF16)

    @pl.when(works)
    def _():
        sent(parts_out, WORKERS - 1, out_sem)
        for o in range(2):

            @pl.when(core == o)
            def _(o=o):
                sent(back_out.at[o], lons - 1, back_send_sem.at[o])

            @pl.when(core != o)
            def _(o=o):
                sent(back_out.at[o], lons, back_send_sem.at[o])

        band_send.wait_send()

    @pl.when(idle)
    def _():
        sent(parts_out, WORKERS, out_sem)

    @pl.when(has_side)
    def _():
        sent(parts_out, WORKERS, side_sem)

    @pl.when(mix_away)
    def _():
        mix_send.wait_send()


def local(latent, lon_filter, mix_weight, band_weight, offsets, w_up, w_down):
    del offsets
    latent, band_weight = jnp.transpose(latent, (1, 0, 2)), jnp.transpose(band_weight, (2, 1, 0))
    count, length = lon_filter.shape
    lons = lax.axis_size("lon")
    channels = w_up.shape[0]
    share = channels // WORKERS
    whole = pl.BlockSpec(memory_space=pltpu.HBM)
    result = pl.pallas_call(
        kernel,
        out_shape=jax.ShapeDtypeStruct(latent.shape, latent.dtype),
        in_specs=[whole] * 6,
        out_specs=pl.BlockSpec(memory_space=pltpu.VMEM),
        scratch_shapes=[
            pltpu.VMEM(latent.shape, BF16),
            pltpu.VMEM(lon_filter.shape, BF16),
            pltpu.VMEM((2, pl.cdiv(count, PACK), PACK_ROWS, LANES), BF16),
            pltpu.VMEM((2, *band_weight.shape), BF16),
            pltpu.VMEM(w_up.shape, BF16),
            pltpu.VMEM(w_down.shape, BF16),
            pltpu.VMEM((channels // LANES, 2 * latent.shape[0], LANES), F32),
            pltpu.VMEM((2 * latent.shape[0], channels), F32),
            pltpu.VMEM(mix_weight.shape, BF16),
            pltpu.VMEM((pl.cdiv(count, PACK), PACK_ROWS, LANES), BF16),
            pltpu.VMEM((WORKERS, 8, LANES), BF16),
            pltpu.VMEM((4, lons, 8, LANES), BF16),
            pltpu.VMEM((2, lons, 8, LANES), BF16),
            pltpu.VMEM((WORKERS, 8, LANES), BF16),
            pltpu.VMEM((4, WIDE, LANES), F32),
            pltpu.VMEM((8 * share, GROUPS * WIDE), F32),
            pltpu.VMEM((GROUPS * WIDE, length), BF16),
            pltpu.VMEM((GROUPS * count * WIDE, length), BF16),
            pltpu.VMEM((share, LANES), F32),
            pltpu.VMEM((2, count * 2 * share, 2 * LANES), BF16),
            pltpu.VMEM((4 * share, length), F32),
            pltpu.VMEM((2, length + 8, LANES), F32),
            pltpu.VMEM((2, length, LANES), F32),
            pltpu.SemaphoreType.DMA((6,)),
            pltpu.SemaphoreType.DMA((2,)),
            pltpu.SemaphoreType.DMA((2,)),
            pltpu.SemaphoreType.DMA,
            pltpu.SemaphoreType.DMA,
            pltpu.SemaphoreType.DMA,
            pltpu.SemaphoreType.DMA((4, GROUPS)),
            pltpu.SemaphoreType.DMA((2,)),
            pltpu.SemaphoreType.DMA,
        ],
        compiler_params=pltpu.CompilerParams(vmem_limit_bytes=16384 << 10, collective_id=0, has_side_effects=True),
    )(*(pltpu.with_memory_space_constraint(x, pltpu.HBM) for x in (latent, lon_filter, mix_weight, band_weight, w_up, w_down)))
    return jnp.transpose(result, (1, 0, 2))


def solution(mesh):
    return jax.shard_map(
        local,
        mesh=mesh,
        in_specs=(
            P("lat", "lon", None),
            P(),
            P(None, "lon", None),
            P(None, "lat", None),
            P("lat"),
            P(),
            P(),
        ),
        out_specs=P("lat", "lon", None),
        check_vma=False,
    )
```

```python
import jax
import jax.numpy as jnp
from jax import lax
from jax.experimental import pallas as pl
from jax.experimental.pallas import tpu as pltpu
from jax.sharding import PartitionSpec as P

MESH = pl.DeviceIdType.MESH
F32 = jnp.float32
BF16 = jnp.bfloat16
X_CHIPS, Z_CHIPS = 4, 8
WORK_Z = 2
WORKERS = X_CHIPS * WORK_Z * 2
SIGNAL_Z = (4, 5, 6, 7, 3, 2, 1, 0)
WORK_AT = [(core, x * Z_CHIPS + z) for x in range(X_CHIPS) for z in range(WORK_Z) for core in range(2)]
LANES = 128
AHEAD = 8
GROUPS = 2
WIDE = 2 * LANES
PACK, PACK_ROWS = 6, 32


def erf_gelu(value):
    return 0.5 * value * (1.0 + lax.erf(value * 0.7071067811865476))


def kernel(
    latent_hbm, filter_hbm, mix_hbm, band_hbm, up_hbm, down_hbm, out_ref,
    latent_in, filter_in, mix_in, band_in, up_in, down_in,
    points, rows, mix_own, mix_out, parts_out, parts_in, back_out, back_in,
    gathered, stack, plain, table, mix_wide, mixer, total, turned, turned_last,
    load_sem, small_send_sem, mix_sem, band_sem, out_sem, side_sem, in_sem, back_send_sem, back_sem,
):
    lat, lon = lax.axis_index("lat"), lax.axis_index("lon")
    lats, lons = lax.axis_size("lat"), lax.axis_size("lon")
    width, _, channels = latent_in.shape
    count, length = filter_in.shape
    group = mix_own.shape[1]
    members = lons // GROUPS
    my_x, my_z = lon // Z_CHIPS, lax.rem(lon, Z_CHIPS)
    my_place = my_z * X_CHIPS + my_x
    my_group = my_place // members
    share = channels // WORKERS
    core = lax.rem(lat, 2)
    base = lat - core
    my_work = (my_x * WORK_Z + my_z) * 2 + core
    works = my_z < WORK_Z
    idle = jnp.logical_not(works)
    has_low, has_high = base > 0, base + 2 < lats
    aside = base + jnp.where(core == 0, -2, 2)
    has_side = jnp.where(core == 0, base > 0, base + 2 < lats)

    def load(source, target, n):
        return pltpu.make_async_copy(source, target, load_sem.at[n])

    latent_load = load(latent_hbm, latent_in, 0)
    filter_load = load(filter_hbm, filter_in, 1)
    band_load = load(band_hbm, band_in.at[core], 2)
    up_load = load(up_hbm, up_in, 3)
    down_load = load(down_hbm, down_in, 4)
    mix_load = load(mix_hbm, mix_own, 5)
    latent_load.start()

    @pl.when(core == 1)
    def _():
        mix_load.start()


    def send(source, target, send_sem, recv_sem, device):
        return pltpu.make_async_remote_copy(
            src_ref=source,
            dst_ref=target,
            send_sem=send_sem,
            recv_sem=recv_sem,
            device_id=device,
            device_id_type=MESH,
        )

    barrier = pltpu.get_barrier_semaphore()

    def signal(to_lat, to_lon):
        pl.semaphore_signal(barrier, inc=1, device_id=(to_lat, to_lon), device_id_type=MESH)

    @pl.when(works)
    def _():
        for z in SIGNAL_Z:
            for x in range(X_CHIPS):
                to_lon = x * Z_CHIPS + z
                for c in range(2):
                    if z < WORK_Z:

                        @pl.when((lon != to_lon) | (core != c))
                        def _(c=c, to_lon=to_lon):
                            signal(base + c, to_lon)
                    else:
                        signal(base + c, to_lon)

            @pl.when(has_high)
            def _(z=z):
                for x in range(X_CHIPS):
                    signal(base + 2, x * Z_CHIPS + z)

            @pl.when(has_low)
            def _(z=z):
                for x in range(X_CHIPS):
                    signal(base - 1, x * Z_CHIPS + z)

    filter_load.start()
    band_load.start()

    pl.semaphore_wait(
        barrier,
        WORKERS - works.astype(jnp.int32) + jnp.where(has_side, WORKERS, 0),
    )

    mix_work = lon // 2
    mix_core = lax.rem(mix_work, 2)
    mix_lon = (mix_work // (2 * WORK_Z)) * Z_CHIPS + lax.rem(mix_work // 2, WORK_Z)
    half = lax.rem(lon, 2)
    mix_send = send(mix_out, mix_in.at[half], small_send_sem.at[0], mix_sem.at[half], (base + mix_core, mix_lon))
    mix_copy = pltpu.make_async_copy(mix_out, mix_in.at[half], mix_sem.at[half])
    band_send = send(band_hbm, band_in.at[core], small_send_sem.at[1], band_sem, (base + 1 - core, lon))
    mix_here = (core == mix_core) & (lon == mix_lon)
    mix_away = (core == 1) & jnp.logical_not(mix_here)

    @pl.when(works)
    def _():
        band_send.start()

    blocks = channels // LANES
    columns = [slice(LANES * t, LANES * (t + 1)) for t in range(blocks)]
    rest = width - AHEAD
    places = [
        (slice(0, AHEAD), pl.ds(0, AHEAD, stride=2)),
        (slice(AHEAD, 2 * AHEAD), pl.ds(1, AHEAD, stride=2)),
        (slice(2 * AHEAD, 2 * AHEAD + rest), pl.ds(2 * AHEAD, rest, stride=2)),
        (slice(2 * AHEAD + rest, 2 * width), pl.ds(2 * AHEAD + 1, rest, stride=2)),
    ]
    latent_load.wait()
    for t, column in enumerate(columns):
        for n in range(width):
            points[t, 2 * n : 2 * n + 2, :] = latent_in[n, :, column].astype(F32)
        for place, point in places:
            rows[place, column] = points[t, point, :]

    lane = lax.broadcasted_iota(jnp.int32, (8, LANES), 1)
    upper = lax.broadcasted_iota(jnp.int32, (8, LANES), 0) < rest
    tiles = [rows[8 * q : 8 * q + 8, :] for q in range(3)]
    tiles[2] = jnp.where(lax.rem(my_x, 2) == 1, pltpu.roll(tiles[2], rest, 0), tiles[2])
    for w in range(WORKERS):
        tile, place = divmod(w * share, LANES)
        message = jnp.zeros((8, LANES), F32)
        for q in range(3):
            piece = tiles[q][:, columns[tile]]
            if place + share > LANES:
                piece = jnp.where(lane >= place, piece, tiles[q][:, columns[tile + 1]])
            shift = (share * q - place) % LANES
            if shift:
                piece = pltpu.roll(piece, shift, 1)
            inside = (lane >= share * q) & (lane < share * (q + 1))
            message = jnp.where(inside, piece, message)
        parts_out[w] = message.astype(BF16)

    @pl.when(works)
    def _():
        parts_in[core + 1, my_place] = parts_out[my_work]

    def send_points(steps):
        for side, z, dx in steps:
            to_x = lax.rem(my_x + dx, X_CHIPS)
            to_lon = to_x * Z_CHIPS + z
            for c in range(2):
                w = (to_x * WORK_Z + z) * 2 + c
                if side:

                    @pl.when(has_side)
                    def _(c=c, w=w, to_lon=to_lon):
                        slot = jnp.where(core == 0, 3, 0)
                        send(
                            parts_out.at[w], parts_in.at[slot, my_place], side_sem, in_sem.at[slot, my_group], (aside + c, to_lon)
                        ).start()
                else:

                    @pl.when((lon != to_lon) | (core != c))
                    def _(c=c, w=w, to_lon=to_lon):
                        send(
                            parts_out.at[w], parts_in.at[core + 1, my_place], out_sem, in_sem.at[core + 1, my_group], (base + c, to_lon)
                        ).start()

    steps = [(side, z, dx) for side in (1, 0) for z in reversed(range(WORK_Z)) for dx in (2, 1, 3, 0)]
    steps.sort(key=lambda s: -(s[0] + s[1] + min(s[2], X_CHIPS - s[2])))
    send_points(steps[: len(steps) // 2])

    @pl.when(core == 1)
    def _():
        mix_load.wait()
        mix_wide[...] = jnp.zeros(mix_wide.shape, F32)
        for first in range(0, count, PACK):
            packed = jnp.zeros((share, LANES), F32)
            for n in range(min(PACK, count - first)):
                mix_wide[0:group, 0:group] = mix_own[first + n].astype(F32)
                packed = packed + (pltpu.roll(mix_wide[...], group * n, 1) if n else mix_wide[...])
            mix_out[first // PACK] = packed[0:PACK_ROWS].astype(BF16)

    @pl.when(mix_away)
    def _():
        mix_send.start()

    @pl.when((core == 1) & mix_here)
    def _():
        mix_copy.start()

    send_points(steps[len(steps) // 2 :])
    up_load.start()
    down_load.start()
    filter_load.wait()
    band_load.wait()

    @pl.when(works)
    def _():
        row8 = lax.broadcasted_iota(jnp.int32, (8, length), 0)
        column_of = lax.broadcasted_iota(jnp.int32, (length, length), 1)
        chip_z, chip_x = column_of // (X_CHIPS * width), lax.rem(column_of // width, X_CHIPS)
        column_of = (chip_x * Z_CHIPS + chip_z) * width + lax.rem(column_of, width)
        order = (column_of == lax.broadcasted_iota(jnp.int32, (length, length), 0)).astype(F32).astype(BF16)
        for g in range(GROUPS):
            plain[WIDE * g + 12 * members : WIDE * (g + 1), :] = jnp.zeros((WIDE - 12 * members, length), BF16)
        filters = filter_in[...].astype(F32)
        for k in range(count):
            first = jnp.broadcast_to(filters[k : k + 1, :], (8, length))
            first = pltpu.roll(first, 0, 1, stride=1, stride_axis=0)
            step = Z_CHIPS * width
            last = jnp.where(row8 < rest, pltpu.roll(first, AHEAD, 1), pltpu.roll(first, AHEAD + step - rest, 1))
            first = jnp.concatenate([first, pltpu.roll(first, step, 1)], axis=0)
            last = jnp.concatenate([last, pltpu.roll(last, 2 * step, 1)], axis=0)
            for z in range(Z_CHIPS):
                g, at = divmod(z * X_CHIPS, members)
                for x in range(0, X_CHIPS, 2):
                    shift = (x * step + z * width) % length
                    turn = pltpu.roll(first, shift, 1) if shift else first
                    row = WIDE * g + 8 * (at + x)
                    plain[row : row + 16, :] = turn.astype(BF16)
                turn = pltpu.roll(last, z * width, 1) if z else last
                row = WIDE * g + 8 * members + 4 * at
                plain[row : row + 16, :] = turn.astype(BF16)
            for g in range(GROUPS):
                top = (g * count + k) * WIDE
                table[top : top + WIDE, :] = jnp.dot(
                    plain[WIDE * g : WIDE * (g + 1), :], order, preferred_element_type=F32
                ).astype(BF16)

        gathered[:, 12 * members :, :] = jnp.zeros((4, WIDE - 12 * members, LANES), F32)

        @pl.when(jnp.logical_not(has_low))
        def _():
            parts_in[0] = jnp.zeros(parts_in.shape[1:], BF16)

        @pl.when(jnp.logical_not(has_high))
        def _():
            parts_in[3] = jnp.zeros(parts_in.shape[1:], BF16)

        def arrive(n, g, some):
            taken = parts_in.at[n, pl.ds(0, some)]
            send(taken, taken, out_sem, in_sem.at[n, g], (base, lon)).wait_recv()

        def unfold(n, g):
            for p in range(members // 2):
                even, odd = (parts_in[n, g * members + 2 * p + m].astype(F32) for m in range(2))
                gathered[n, 16 * p : 16 * p + 8, :] = even
                gathered[n, 16 * p + 8 : 16 * p + 16, :] = odd
                one = pltpu.roll(jnp.where(upper, odd, even), rest, 0)
                one = pltpu.roll(one, LANES - share, 1)
                zero = pltpu.roll(jnp.where(upper, even, odd), LANES - 2 * share, 1)
                row = 8 * members + 8 * p
                gathered[n, row : row + 8, :] = jnp.where(lane < share, zero, one)
            stack[2 * share * n : 2 * share * (n + 1), WIDE * g : WIDE * (g + 1)] = gathered[n].T[0 : 2 * share]

        def take(g):
            for n, there in ((0, has_low), (3, has_high)):

                @pl.when(there)
                def _(n=n):
                    arrive(n, g, members)

            for n in (1, 2):
                if g * members < WORK_Z * X_CHIPS:
                    own = (core + 1 == n) & (my_group == g)

                    @pl.when(own)
                    def _(n=n):
                        arrive(n, g, members - 1)

                    @pl.when(jnp.logical_not(own))
                    def _(n=n):
                        arrive(n, g, members)
                else:
                    arrive(n, g, members)
            for n in range(4):
                unfold(n, g)

        def mix(g):
            pad = jnp.zeros((LANES - 3 * share, WIDE), F32)
            lanes = slice(WIDE * g, WIDE * (g + 1))
            sides = []
            for o in range(2):
                top = 2 * share * o
                wide = jnp.concatenate(
                    [stack[top : top + 3 * share, lanes], pad, stack[top + 3 * share : top + 6 * share, lanes], pad],
                    axis=0,
                ).astype(BF16)
                mixed = jnp.dot(mixer[o], wide, preferred_element_type=F32).astype(BF16)
                sides.append(
                    jnp.concatenate([mixed[2 * share * k : 2 * share * (k + 1), :] for k in range(count)], axis=1)
                )
            return jnp.concatenate(sides, axis=0)

        def part(g, start, end):
            return table[count * WIDE * g : count * WIDE * (g + 1), start:end]

        take(0)

        for h in range(2):
            send(mix_out, mix_in.at[h], small_send_sem.at[0], mix_sem.at[h], (base, lon)).wait_recv()
        band_send.wait_recv()
        third = lax.broadcasted_iota(jnp.int32, (1, LANES), 1) // share
        wide_lane = lax.broadcasted_iota(jnp.int32, (PACK_ROWS, LANES), 1)
        bands = [band_in[o].astype(F32) for o in range(2)]
        empty = jnp.zeros((share, LANES), F32)
        for k in range(count):
            for h in range(2):
                shift = (group * h - group * (k % PACK)) % LANES
                once = mix_in[h, k // PACK].astype(F32)
                once = pltpu.roll(once, shift, 1) if shift else once
                once = jnp.where((wide_lane >= group * h) & (wide_lane < group * (h + 1)), once, 0.0)
                mix_wide[group * h : group * (h + 1), :] = once[0:group]
            once = mix_wide[...]
            every = once + pltpu.roll(once, share, 1) + pltpu.roll(once, 2 * share, 1)
            for o in range(2):
                scaled = []
                for i in range(2):
                    scale = jnp.zeros((1, LANES), F32)
                    for t in range(3):
                        scale = jnp.where(third == t, bands[o][t, i : i + 1, k : k + 1], scale)
                    scaled.append(every * scale)
                whole = jnp.concatenate(
                    [
                        jnp.concatenate([scaled[0], empty], axis=1),
                        jnp.concatenate([empty, scaled[1]], axis=1),
                    ],
                    axis=0,
                )
                mixer[o, 2 * share * k : 2 * share * (k + 1), :] = whole.astype(BF16)

        total[...] = jnp.dot(mix(0), part(0, 0, length), preferred_element_type=F32)
        turned[:, length:, :] = jnp.zeros((2, turned.shape[1] - length, LANES), F32)
        take(1)
        late = mix(1)

        def finish(start, end, chips):
            convolved = total[:, start:end] + jnp.dot(late, part(1, start, end), preferred_element_type=F32)
            fill = jnp.zeros((LANES - 3 * share, end - start), F32)
            for o in range(2):
                one = convolved[2 * share * o : 2 * share * (o + 1), :]
                one = jnp.concatenate([one, one[0:share], fill], axis=0).T
                turned[o, start:end, :] = one
                turned_last[o, start:end, :] = pltpu.roll(one, share, 1)
            for z in chips:
                for x in range(X_CHIPS):
                    b, at = x * Z_CHIPS + z, (z * X_CHIPS + x) * width
                    for o in range(2):
                        begin = turned[o, at : at + 8, :]
                        end0 = turned[o, at + AHEAD : at + AHEAD + 8, :]
                        end1 = turned_last[o, at + rest : at + rest + 8, :]
                        message = jnp.where(lane < 2 * share, begin, jnp.where(upper, end0, end1))
                        back_out[o, b] = message.astype(BF16)
            for z in chips:
                for x in range(X_CHIPS):
                    b = x * Z_CHIPS + z
                    for o in range(2):
                        back = send(back_out.at[o, b], back_in.at[my_work], back_send_sem.at[o], back_sem, (base + o, b))
                        if z < WORK_Z:

                            @pl.when((lon != b) | (core != o))
                            def _(back=back):
                                back.start()
                        else:
                            back.start()

        finish(0, LANES, range(WORK_Z))
        back_in[my_work] = back_out[core, lon]
        finish(LANES, length, range(WORK_Z, Z_CHIPS))

    def sent(buffer, members, sem):
        taken = buffer.at[pl.ds(0, members)]
        send(taken, taken, sem, back_sem, (lat, 0)).wait_send()

    def returned(members):
        taken = back_in.at[pl.ds(0, members)]
        send(taken, taken, out_sem, back_sem, (lat, 0)).wait_recv()

    up_load.wait()
    down_load.wait()

    @pl.when(works)
    def _():
        returned(WORKERS - 1)

    @pl.when(idle)
    def _():
        returned(WORKERS)

    sums = [[jnp.zeros((8, LANES), F32) for _ in range(blocks)] for _ in range(3)]
    for w in range(WORKERS):
        tile, place = divmod(w * share, LANES)
        message = back_in[w].astype(F32)
        for q in range(3):
            shift = (place - share * q) % LANES
            piece = pltpu.roll(message, shift, 1) if shift else message
            inside = (lane >= place) & (lane < place + share)
            sums[q][tile] = jnp.where(inside, piece, sums[q][tile])
            if place + share > LANES:
                sums[q][tile + 1] = jnp.where(lane < place + share - LANES, piece, sums[q][tile + 1])
    returned_rows = jnp.concatenate([jnp.concatenate(one, axis=1) for one in sums], axis=0)

    summed = (rows[...] + returned_rows).astype(BF16).astype(F32)
    mean = jnp.mean(summed, axis=1, keepdims=True)
    centred = summed - mean
    var = jnp.mean(centred * centred, axis=1, keepdims=True)
    normed = (centred * lax.rsqrt(var + 1e-05)).astype(BF16)
    hidden = erf_gelu(jnp.dot(normed, up_in[...], preferred_element_type=F32)).astype(BF16)
    result = summed + jnp.dot(hidden, down_in[...], preferred_element_type=F32)
    for t, column in enumerate(columns):
        for place, point in places:
            points[t, point, :] = result[place, column]
        for n in range(width):
            out_ref[n, :, column] = points[t, 2 * n : 2 * n + 2, :].astype(BF16)

    @pl.when(works)
    def _():
        sent(parts_out, WORKERS - 1, out_sem)
        for o in range(2):

            @pl.when(core == o)
            def _(o=o):
                sent(back_out.at[o], lons - 1, back_send_sem.at[o])

            @pl.when(core != o)
            def _(o=o):
                sent(back_out.at[o], lons, back_send_sem.at[o])

        band_send.wait_send()

    @pl.when(idle)
    def _():
        sent(parts_out, WORKERS, out_sem)

    @pl.when(has_side)
    def _():
        sent(parts_out, WORKERS, side_sem)

    @pl.when(mix_away)
    def _():
        mix_send.wait_send()


def local(latent, lon_filter, mix_weight, band_weight, offsets, w_up, w_down):
    del offsets
    latent, band_weight = jnp.transpose(latent, (1, 0, 2)), jnp.transpose(band_weight, (2, 1, 0))
    count, length = lon_filter.shape
    lons = lax.axis_size("lon")
    channels = w_up.shape[0]
    share = channels // WORKERS
    whole = pl.BlockSpec(memory_space=pltpu.HBM)
    result = pl.pallas_call(
        kernel,
        out_shape=jax.ShapeDtypeStruct(latent.shape, latent.dtype),
        in_specs=[whole] * 6,
        out_specs=pl.BlockSpec(memory_space=pltpu.VMEM),
        scratch_shapes=[
            pltpu.VMEM(latent.shape, BF16),
            pltpu.VMEM(lon_filter.shape, BF16),
            pltpu.VMEM((2, pl.cdiv(count, PACK), PACK_ROWS, LANES), BF16),
            pltpu.VMEM((2, *band_weight.shape), BF16),
            pltpu.VMEM(w_up.shape, BF16),
            pltpu.VMEM(w_down.shape, BF16),
            pltpu.VMEM((channels // LANES, 2 * latent.shape[0], LANES), F32),
            pltpu.VMEM((2 * latent.shape[0], channels), F32),
            pltpu.VMEM(mix_weight.shape, BF16),
            pltpu.VMEM((pl.cdiv(count, PACK), PACK_ROWS, LANES), BF16),
            pltpu.VMEM((WORKERS, 8, LANES), BF16),
            pltpu.VMEM((4, lons, 8, LANES), BF16),
            pltpu.VMEM((2, lons, 8, LANES), BF16),
            pltpu.VMEM((WORKERS, 8, LANES), BF16),
            pltpu.VMEM((4, WIDE, LANES), F32),
            pltpu.VMEM((8 * share, GROUPS * WIDE), F32),
            pltpu.VMEM((GROUPS * WIDE, length), BF16),
            pltpu.VMEM((GROUPS * count * WIDE, length), BF16),
            pltpu.VMEM((share, LANES), F32),
            pltpu.VMEM((2, count * 2 * share, 2 * LANES), BF16),
            pltpu.VMEM((4 * share, length), F32),
            pltpu.VMEM((2, length + 8, LANES), F32),
            pltpu.VMEM((2, length, LANES), F32),
            pltpu.SemaphoreType.DMA((6,)),
            pltpu.SemaphoreType.DMA((2,)),
            pltpu.SemaphoreType.DMA((2,)),
            pltpu.SemaphoreType.DMA,
            pltpu.SemaphoreType.DMA,
            pltpu.SemaphoreType.DMA,
            pltpu.SemaphoreType.DMA((4, GROUPS)),
            pltpu.SemaphoreType.DMA((2,)),
            pltpu.SemaphoreType.DMA,
        ],
        compiler_params=pltpu.CompilerParams(vmem_limit_bytes=16384 << 10, collective_id=0, has_side_effects=True),
    )(*(pltpu.with_memory_space_constraint(x, pltpu.HBM) for x in (latent, lon_filter, mix_weight, band_weight, w_up, w_down)))
    return jnp.transpose(result, (1, 0, 2))


def solution(mesh):
    return jax.shard_map(
        local,
        mesh=mesh,
        in_specs=(
            P("lat", "lon", None),
            P(),
            P(None, "lon", None),
            P(None, "lat", None),
            P("lat"),
            P(),
            P(),
        ),
        out_specs=P("lat", "lon", None),
        check_vma=False,
    )
```

```python
import jax
import jax.numpy as jnp
from jax import lax
from jax.experimental import pallas as pl
from jax.experimental.pallas import tpu as pltpu
from jax.sharding import PartitionSpec as P

MESH = pl.DeviceIdType.MESH
F32 = jnp.float32
BF16 = jnp.bfloat16
X_CHIPS, Z_CHIPS = 4, 8
WORK_Z = 2
WORKERS = X_CHIPS * WORK_Z * 2
SIGNAL_Z = (4, 5, 6, 7, 3, 2, 1, 0)
WORK_AT = [(core, x * Z_CHIPS + z) for x in range(X_CHIPS) for z in range(WORK_Z) for core in range(2)]
LANES = 128
AHEAD = 8
GROUPS = 2
WIDE = 2 * LANES
PACK, PACK_ROWS = 6, 32


def erf_gelu(value):
    return 0.5 * value * (1.0 + lax.erf(value * 0.7071067811865476))


def kernel(
    latent_hbm, filter_hbm, mix_hbm, band_hbm, up_hbm, down_hbm, out_ref,
    latent_in, filter_in, mix_in, band_in, up_in, down_in,
    points, rows, mix_own, mix_out, parts_out, parts_in, back_out, back_in,
    gathered, stack, plain, table, mix_wide, mixer, total, turned, turned_last,
    load_sem, small_send_sem, mix_sem, band_sem, out_sem, side_sem, in_sem, back_send_sem, back_sem,
):
    lat, lon = lax.axis_index("lat"), lax.axis_index("lon")
    lats, lons = lax.axis_size("lat"), lax.axis_size("lon")
    width, _, channels = latent_in.shape
    count, length = filter_in.shape
    group = mix_own.shape[1]
    members = lons // GROUPS
    my_x, my_z = lon // Z_CHIPS, lax.rem(lon, Z_CHIPS)
    my_place = my_z * X_CHIPS + my_x
    my_group = my_place // members
    share = channels // WORKERS
    core = lax.rem(lat, 2)
    base = lat - core
    my_work = (my_x * WORK_Z + my_z) * 2 + core
    works = my_z < WORK_Z
    idle = jnp.logical_not(works)
    has_low, has_high = base > 0, base + 2 < lats
    aside = base + jnp.where(core == 0, -2, 2)
    has_side = jnp.where(core == 0, base > 0, base + 2 < lats)

    def load(source, target, n):
        return pltpu.make_async_copy(source, target, load_sem.at[n])

    latent_load = load(latent_hbm, latent_in, 0)
    filter_load = load(filter_hbm, filter_in, 1)
    band_load = load(band_hbm, band_in.at[core], 2)
    up_load = load(up_hbm, up_in, 3)
    down_load = load(down_hbm, down_in, 4)
    mix_load = load(mix_hbm, mix_own, 5)
    latent_load.start()

    @pl.when(core == 1)
    def _():
        mix_load.start()


    def send(source, target, send_sem, recv_sem, device):
        return pltpu.make_async_remote_copy(
            src_ref=source,
            dst_ref=target,
            send_sem=send_sem,
            recv_sem=recv_sem,
            device_id=device,
            device_id_type=MESH,
        )

    barrier = pltpu.get_barrier_semaphore()

    def signal(to_lat, to_lon):
        pl.semaphore_signal(barrier, inc=1, device_id=(to_lat, to_lon), device_id_type=MESH)

    @pl.when(works)
    def _():
        for z in SIGNAL_Z:
            for x in range(X_CHIPS):
                to_lon = x * Z_CHIPS + z
                for c in range(2):
                    if z < WORK_Z:

                        @pl.when((lon != to_lon) | (core != c))
                        def _(c=c, to_lon=to_lon):
                            signal(base + c, to_lon)
                    else:
                        signal(base + c, to_lon)

            @pl.when(has_high)
            def _(z=z):
                for x in range(X_CHIPS):
                    signal(base + 2, x * Z_CHIPS + z)

            @pl.when(has_low)
            def _(z=z):
                for x in range(X_CHIPS):
                    signal(base - 1, x * Z_CHIPS + z)

    filter_load.start()
    band_load.start()

    pl.semaphore_wait(
        barrier,
        WORKERS - works.astype(jnp.int32) + jnp.where(has_side, WORKERS, 0),
    )

    mix_work = lon // 2
    mix_core = lax.rem(mix_work, 2)
    mix_lon = (mix_work // (2 * WORK_Z)) * Z_CHIPS + lax.rem(mix_work // 2, WORK_Z)
    half = lax.rem(lon, 2)
    mix_send = send(mix_out, mix_in.at[half], small_send_sem.at[0], mix_sem.at[half], (base + mix_core, mix_lon))
    mix_copy = pltpu.make_async_copy(mix_out, mix_in.at[half], mix_sem.at[half])
    band_send = send(band_hbm, band_in.at[core], small_send_sem.at[1], band_sem, (base + 1 - core, lon))
    mix_here = (core == mix_core) & (lon == mix_lon)
    mix_away = (core == 1) & jnp.logical_not(mix_here)

    @pl.when(works)
    def _():
        band_send.start()

    blocks = channels // LANES
    columns = [slice(LANES * t, LANES * (t + 1)) for t in range(blocks)]
    rest = width - AHEAD
    places = [
        (slice(0, AHEAD), pl.ds(0, AHEAD, stride=2)),
        (slice(AHEAD, 2 * AHEAD), pl.ds(1, AHEAD, stride=2)),
        (slice(2 * AHEAD, 2 * AHEAD + rest), pl.ds(2 * AHEAD, rest, stride=2)),
        (slice(2 * AHEAD + rest, 2 * width), pl.ds(2 * AHEAD + 1, rest, stride=2)),
    ]
    latent_load.wait()
    for t, column in enumerate(columns):
        for n in range(width):
            points[t, 2 * n : 2 * n + 2, :] = latent_in[n, :, column].astype(F32)
        for place, point in places:
            rows[place, column] = points[t, point, :]

    lane = lax.broadcasted_iota(jnp.int32, (8, LANES), 1)
    upper = lax.broadcasted_iota(jnp.int32, (8, LANES), 0) < rest
    tiles = [rows[8 * q : 8 * q + 8, :] for q in range(3)]
    tiles[2] = jnp.where(lax.rem(my_x, 2) == 1, pltpu.roll(tiles[2], rest, 0), tiles[2])
    for w in range(WORKERS):
        tile, place = divmod(w * share, LANES)
        message = jnp.zeros((8, LANES), F32)
        for q in range(3):
            piece = tiles[q][:, columns[tile]]
            if place + share > LANES:
                piece = jnp.where(lane >= place, piece, tiles[q][:, columns[tile + 1]])
            shift = (share * q - place) % LANES
            if shift:
                piece = pltpu.roll(piece, shift, 1)
            inside = (lane >= share * q) & (lane < share * (q + 1))
            message = jnp.where(inside, piece, message)
        parts_out[w] = message.astype(BF16)

    @pl.when(works)
    def _():
        parts_in[core + 1, my_place] = parts_out[my_work]

    def send_points(steps):
        for side, z, dx in steps:
            to_x = lax.rem(my_x + dx, X_CHIPS)
            to_lon = to_x * Z_CHIPS + z
            for c in range(2):
                w = (to_x * WORK_Z + z) * 2 + c
                if side:

                    @pl.when(has_side)
                    def _(c=c, w=w, to_lon=to_lon):
                        slot = jnp.where(core == 0, 3, 0)
                        send(
                            parts_out.at[w], parts_in.at[slot, my_place], side_sem, in_sem.at[slot, my_group], (aside + c, to_lon)
                        ).start()
                else:

                    @pl.when((lon != to_lon) | (core != c))
                    def _(c=c, w=w, to_lon=to_lon):
                        send(
                            parts_out.at[w], parts_in.at[core + 1, my_place], out_sem, in_sem.at[core + 1, my_group], (base + c, to_lon)
                        ).start()

    steps = [(side, z, dx) for side in (1, 0) for z in reversed(range(WORK_Z)) for dx in (2, 1, 3, 0)]
    steps.sort(key=lambda s: -(s[0] + s[1] + min(s[2], X_CHIPS - s[2])))
    send_points(steps[: len(steps) // 2])

    @pl.when(core == 1)
    def _():
        mix_load.wait()
        mix_wide[...] = jnp.zeros(mix_wide.shape, F32)
        for first in range(0, count, PACK):
            packed = jnp.zeros((share, LANES), F32)
            for n in range(min(PACK, count - first)):
                mix_wide[0:group, 0:group] = mix_own[first + n].astype(F32)
                once = mix_wide[0:share, :]
                packed = packed + (pltpu.roll(once, group * n, 1) if n else once)
            mix_out[first // PACK] = packed[0:PACK_ROWS].astype(BF16)

    @pl.when(mix_away)
    def _():
        mix_send.start()

    @pl.when((core == 1) & mix_here)
    def _():
        mix_copy.start()

    send_points(steps[len(steps) // 2 :])
    up_load.start()
    down_load.start()
    filter_load.wait()
    band_load.wait()

    @pl.when(works)
    def _():
        row8 = lax.broadcasted_iota(jnp.int32, (8, length), 0)
        column_of = lax.broadcasted_iota(jnp.int32, (length, length), 1)
        chip_z, chip_x = column_of // (X_CHIPS * width), lax.rem(column_of // width, X_CHIPS)
        column_of = (chip_x * Z_CHIPS + chip_z) * width + lax.rem(column_of, width)
        order = (column_of == lax.broadcasted_iota(jnp.int32, (length, length), 0)).astype(F32).astype(BF16)
        for g in range(GROUPS):
            plain[WIDE * g + 12 * members : WIDE * (g + 1), :] = jnp.zeros((WIDE - 12 * members, length), BF16)
        filters = filter_in[...].astype(F32)
        for k in range(count):
            first = jnp.broadcast_to(filters[k : k + 1, :], (8, length))
            first = pltpu.roll(first, 0, 1, stride=1, stride_axis=0)
            step = Z_CHIPS * width
            last = jnp.where(row8 < rest, pltpu.roll(first, AHEAD, 1), pltpu.roll(first, AHEAD + step - rest, 1))
            first = jnp.concatenate([first, pltpu.roll(first, step, 1)], axis=0)
            last = jnp.concatenate([last, pltpu.roll(last, 2 * step, 1)], axis=0)
            for z in range(Z_CHIPS):
                g, at = divmod(z * X_CHIPS, members)
                for x in range(0, X_CHIPS, 2):
                    shift = (x * step + z * width) % length
                    turn = pltpu.roll(first, shift, 1) if shift else first
                    row = WIDE * g + 8 * (at + x)
                    plain[row : row + 16, :] = turn.astype(BF16)
                turn = pltpu.roll(last, z * width, 1) if z else last
                row = WIDE * g + 8 * members + 4 * at
                plain[row : row + 16, :] = turn.astype(BF16)
            for g in range(GROUPS):
                top = (g * count + k) * WIDE
                table[top : top + WIDE, :] = jnp.dot(
                    plain[WIDE * g : WIDE * (g + 1), :], order, preferred_element_type=F32
                ).astype(BF16)

        gathered[:, 12 * members :, :] = jnp.zeros((4, WIDE - 12 * members, LANES), F32)

        @pl.when(jnp.logical_not(has_low))
        def _():
            parts_in[0] = jnp.zeros(parts_in.shape[1:], BF16)

        @pl.when(jnp.logical_not(has_high))
        def _():
            parts_in[3] = jnp.zeros(parts_in.shape[1:], BF16)

        def arrive(n, g, some):
            taken = parts_in.at[n, pl.ds(0, some)]
            send(taken, taken, out_sem, in_sem.at[n, g], (base, lon)).wait_recv()

        def unfold(n, g):
            for p in range(members // 2):
                even, odd = (parts_in[n, g * members + 2 * p + m].astype(F32) for m in range(2))
                gathered[n, 16 * p : 16 * p + 8, :] = even
                gathered[n, 16 * p + 8 : 16 * p + 16, :] = odd
                one = pltpu.roll(jnp.where(upper, odd, even), rest, 0)
                one = pltpu.roll(one, LANES - share, 1)
                zero = pltpu.roll(jnp.where(upper, even, odd), LANES - 2 * share, 1)
                row = 8 * members + 8 * p
                gathered[n, row : row + 8, :] = jnp.where(lane < share, zero, one)
            stack[2 * share * n : 2 * share * (n + 1), WIDE * g : WIDE * (g + 1)] = gathered[n].T[0 : 2 * share]

        def take(g):
            for n, there in ((0, has_low), (3, has_high)):

                @pl.when(there)
                def _(n=n):
                    arrive(n, g, members)

            for n in (1, 2):
                if g * members < WORK_Z * X_CHIPS:
                    own = (core + 1 == n) & (my_group == g)

                    @pl.when(own)
                    def _(n=n):
                        arrive(n, g, members - 1)

                    @pl.when(jnp.logical_not(own))
                    def _(n=n):
                        arrive(n, g, members)
                else:
                    arrive(n, g, members)
            for n in range(4):
                unfold(n, g)

        def mix(g):
            pad = jnp.zeros((LANES - 3 * share, WIDE), F32)
            lanes = slice(WIDE * g, WIDE * (g + 1))
            sides = []
            for o in range(2):
                top = 2 * share * o
                wide = jnp.concatenate(
                    [stack[top : top + 3 * share, lanes], pad, stack[top + 3 * share : top + 6 * share, lanes], pad],
                    axis=0,
                ).astype(BF16)
                mixed = jnp.dot(mixer[o], wide, preferred_element_type=F32).astype(BF16)
                sides.append(
                    jnp.concatenate([mixed[2 * share * k : 2 * share * (k + 1), :] for k in range(count)], axis=1)
                )
            return jnp.concatenate(sides, axis=0)

        def part(g, start, end):
            return table[count * WIDE * g : count * WIDE * (g + 1), start:end]

        take(0)

        for h in range(2):
            send(mix_out, mix_in.at[h], small_send_sem.at[0], mix_sem.at[h], (base, lon)).wait_recv()
        band_send.wait_recv()
        third = lax.broadcasted_iota(jnp.int32, (1, LANES), 1) // share
        wide_lane = lax.broadcasted_iota(jnp.int32, (PACK_ROWS, LANES), 1)
        bands = [band_in[o].astype(F32) for o in range(2)]
        empty = jnp.zeros((share, LANES), F32)
        for k in range(count):
            for h in range(2):
                shift = (group * h - group * (k % PACK)) % LANES
                once = mix_in[h, k // PACK].astype(F32)
                once = pltpu.roll(once, shift, 1) if shift else once
                once = jnp.where((wide_lane >= group * h) & (wide_lane < group * (h + 1)), once, 0.0)
                mix_wide[group * h : group * (h + 1), :] = once[0:group]
            once = mix_wide[0:share, :]
            every = once + pltpu.roll(once, share, 1) + pltpu.roll(once, 2 * share, 1)
            for o in range(2):
                scaled = []
                for i in range(2):
                    scale = jnp.zeros((1, LANES), F32)
                    for t in range(3):
                        scale = jnp.where(third == t, bands[o][t, i : i + 1, k : k + 1], scale)
                    scaled.append(every * scale)
                whole = jnp.concatenate(
                    [
                        jnp.concatenate([scaled[0], empty], axis=1),
                        jnp.concatenate([empty, scaled[1]], axis=1),
                    ],
                    axis=0,
                )
                mixer[o, 2 * share * k : 2 * share * (k + 1), :] = whole.astype(BF16)

        total[...] = jnp.dot(mix(0), part(0, 0, length), preferred_element_type=F32)
        turned[:, length:, :] = jnp.zeros((2, turned.shape[1] - length, LANES), F32)
        take(1)
        late = mix(1)

        def finish(start, end, chips):
            convolved = total[:, start:end] + jnp.dot(late, part(1, start, end), preferred_element_type=F32)
            fill = jnp.zeros((LANES - 3 * share, end - start), F32)
            for o in range(2):
                one = convolved[2 * share * o : 2 * share * (o + 1), :]
                one = jnp.concatenate([one, one[0:share], fill], axis=0).T
                turned[o, start:end, :] = one
                turned_last[o, start:end, :] = pltpu.roll(one, share, 1)
            for z in chips:
                for x in range(X_CHIPS):
                    b, at = x * Z_CHIPS + z, (z * X_CHIPS + x) * width
                    for o in range(2):
                        begin = turned[o, at : at + 8, :]
                        end0 = turned[o, at + AHEAD : at + AHEAD + 8, :]
                        end1 = turned_last[o, at + rest : at + rest + 8, :]
                        message = jnp.where(lane < 2 * share, begin, jnp.where(upper, end0, end1))
                        back_out[o, b] = message.astype(BF16)
            for z in chips:
                for x in range(X_CHIPS):
                    b = x * Z_CHIPS + z
                    for o in range(2):
                        back = send(back_out.at[o, b], back_in.at[my_work], back_send_sem.at[o], back_sem, (base + o, b))
                        if z < WORK_Z:

                            @pl.when((lon != b) | (core != o))
                            def _(back=back):
                                back.start()
                        else:
                            back.start()

        finish(0, LANES, range(WORK_Z))
        back_in[my_work] = back_out[core, lon]
        finish(LANES, length, range(WORK_Z, Z_CHIPS))

    def sent(buffer, members, sem):
        taken = buffer.at[pl.ds(0, members)]
        send(taken, taken, sem, back_sem, (lat, 0)).wait_send()

    def returned(members):
        taken = back_in.at[pl.ds(0, members)]
        send(taken, taken, out_sem, back_sem, (lat, 0)).wait_recv()

    up_load.wait()
    down_load.wait()

    @pl.when(works)
    def _():
        returned(WORKERS - 1)

    @pl.when(idle)
    def _():
        returned(WORKERS)

    sums = [[jnp.zeros((8, LANES), F32) for _ in range(blocks)] for _ in range(3)]
    for w in range(WORKERS):
        tile, place = divmod(w * share, LANES)
        message = back_in[w].astype(F32)
        for q in range(3):
            shift = (place - share * q) % LANES
            piece = pltpu.roll(message, shift, 1) if shift else message
            inside = (lane >= place) & (lane < place + share)
            sums[q][tile] = jnp.where(inside, piece, sums[q][tile])
            if place + share > LANES:
                sums[q][tile + 1] = jnp.where(lane < place + share - LANES, piece, sums[q][tile + 1])
    returned_rows = jnp.concatenate([jnp.concatenate(one, axis=1) for one in sums], axis=0)

    summed = (rows[0 : 2 * width, :] + returned_rows).astype(BF16).astype(F32)
    mean = jnp.mean(summed, axis=1, keepdims=True)
    centred = summed - mean
    var = jnp.mean(centred * centred, axis=1, keepdims=True)
    normed = (centred * lax.rsqrt(var + 1e-05)).astype(BF16)
    hidden = erf_gelu(jnp.dot(normed, up_in[...], preferred_element_type=F32)).astype(BF16)
    result = summed + jnp.dot(hidden, down_in[...], preferred_element_type=F32)
    for t, column in enumerate(columns):
        for place, point in places:
            points[t, point, :] = result[place, column]
        for n in range(width):
            out_ref[n, :, column] = points[t, 2 * n : 2 * n + 2, :].astype(BF16)

    @pl.when(works)
    def _():
        sent(parts_out, WORKERS - 1, out_sem)
        for o in range(2):

            @pl.when(core == o)
            def _(o=o):
                sent(back_out.at[o], lons - 1, back_send_sem.at[o])

            @pl.when(core != o)
            def _(o=o):
                sent(back_out.at[o], lons, back_send_sem.at[o])

        band_send.wait_send()

    @pl.when(idle)
    def _():
        sent(parts_out, WORKERS, out_sem)

    @pl.when(has_side)
    def _():
        sent(parts_out, WORKERS, side_sem)

    @pl.when(mix_away)
    def _():
        mix_send.wait_send()


def local(latent, lon_filter, mix_weight, band_weight, offsets, w_up, w_down):
    del offsets
    latent, band_weight = jnp.transpose(latent, (1, 0, 2)), jnp.transpose(band_weight, (2, 1, 0))
    count, length = lon_filter.shape
    lons = lax.axis_size("lon")
    channels = w_up.shape[0]
    share = channels // WORKERS
    whole = pl.BlockSpec(memory_space=pltpu.HBM)
    result = pl.pallas_call(
        kernel,
        out_shape=jax.ShapeDtypeStruct(latent.shape, latent.dtype),
        in_specs=[whole] * 6,
        out_specs=pl.BlockSpec(memory_space=pltpu.VMEM),
        scratch_shapes=[
            pltpu.VMEM(latent.shape, BF16),
            pltpu.VMEM(lon_filter.shape, BF16),
            pltpu.VMEM((2, pl.cdiv(count, PACK), PACK_ROWS, LANES), BF16),
            pltpu.VMEM((2, *band_weight.shape), BF16),
            pltpu.VMEM(w_up.shape, BF16),
            pltpu.VMEM(w_down.shape, BF16),
            pltpu.VMEM((channels // LANES, 2 * latent.shape[0] + 8, LANES), F32),
            pltpu.VMEM((2 * latent.shape[0] + 8, channels), F32),
            pltpu.VMEM(mix_weight.shape, BF16),
            pltpu.VMEM((pl.cdiv(count, PACK), PACK_ROWS, LANES), BF16),
            pltpu.VMEM((WORKERS, 8, LANES), BF16),
            pltpu.VMEM((4, lons, 8, LANES), BF16),
            pltpu.VMEM((2, lons, 8, LANES), BF16),
            pltpu.VMEM((WORKERS, 8, LANES), BF16),
            pltpu.VMEM((4, WIDE, LANES), F32),
            pltpu.VMEM((8 * share, GROUPS * WIDE), F32),
            pltpu.VMEM((GROUPS * WIDE, length), BF16),
            pltpu.VMEM((GROUPS * count * WIDE, length), BF16),
            pltpu.VMEM((share + 8, LANES), F32),
            pltpu.VMEM((2, count * 2 * share, 2 * LANES), BF16),
            pltpu.VMEM((4 * share, length), F32),
            pltpu.VMEM((2, length + 8, LANES), F32),
            pltpu.VMEM((2, length, LANES), F32),
            pltpu.SemaphoreType.DMA((6,)),
            pltpu.SemaphoreType.DMA((2,)),
            pltpu.SemaphoreType.DMA((2,)),
            pltpu.SemaphoreType.DMA,
            pltpu.SemaphoreType.DMA,
            pltpu.SemaphoreType.DMA,
            pltpu.SemaphoreType.DMA((4, GROUPS)),
            pltpu.SemaphoreType.DMA((2,)),
            pltpu.SemaphoreType.DMA,
        ],
        compiler_params=pltpu.CompilerParams(vmem_limit_bytes=16384 << 10, collective_id=0, has_side_effects=True),
    )(*(pltpu.with_memory_space_constraint(x, pltpu.HBM) for x in (latent, lon_filter, mix_weight, band_weight, w_up, w_down)))
    return jnp.transpose(result, (1, 0, 2))


def solution(mesh):
    return jax.shard_map(
        local,
        mesh=mesh,
        in_specs=(
            P("lat", "lon", None),
            P(),
            P(None, "lon", None),
            P(None, "lat", None),
            P("lat"),
            P(),
            P(),
        ),
        out_specs=P("lat", "lon", None),
        check_vma=False,
    )
```
